32 devices in a mesh: gx: 4 (over y, core), gy: 4 (over z), frame: 2 (over x).
Axes of the slice: x: 2, y: 2, z: 4, core: 2. Of those that a mesh axis runs over, the one named last changes fastest.
Arguments:
- features: bfloat16 [8, 8, 128, 128], P(('frame', 'gx'), 'gy'), parts along dimension 0, may hold values from -6 to 6
- positions: float32 [8, 8, 3, 128], P(('frame', 'gx'), 'gy'), parts along dimension 0, may hold values from 0 to 1
- bead_types: int32 [8, 8, 128], P(('frame', 'gx'), 'gy'), parts along dimension 0, may hold values from 0 to 15
- cell_counts: int32 [8, 8], P(('frame', 'gx'), 'gy'), parts along dimension 0, may hold values from 48 to 128
- w_value: bfloat16 [128, 128], replicated, may hold values from -0.5 to 0.5
- w_radial: float32 [8, 128], replicated, may hold values from -0.6 to 0.6
- type_gain: float32 [16, 128], replicated, may hold values from 0.1 to 1.9
- w_out: bfloat16 [128, 128], replicated, may hold values from -0.5 to 0.5
- cotangent: bfloat16 [8, 8, 128, 128], P(('frame', 'gx'), 'gy'), parts along dimension 0, may hold values from -6 to 6
Outputs:
- out_feat: bfloat16 [8, 8, 128, 128], P(('frame', 'gx'), 'gy'), parts along dimension 0
- grad_feat: bfloat16 [8, 8, 128, 128], P(('frame', 'gx'), 'gy'), parts along dimension 0
- grad_pos: float32 [8, 8, 3, 128], P(('frame', 'gx'), 'gy'), parts along dimension 0
- grad_wvalue: float32 [256, 128], P('frame'), parts along dimension 0
- grad_wradial: float32 [16, 128], P('frame'), parts along dimension 0
- grad_gain: float32 [32, 128], P('frame'), parts along dimension 0
- grad_wout: float32 [256, 128], P('frame'), parts along dimension 0
The draws below stay inside these ranges and needn't reach their ends.
There are 2 independent parts, one for each index of `frame`. The reference program is written for one: setup_inputs(seed, part) draws one part's arguments, and reference() takes and returns one part's arrays. A program takes and returns all parts, laid end to end along the dimension named above; an argument that names none is the same for every part. Nothing has to cross between parts.
All inputs are finite; a program needn't handle non-finite values.
Results may differ from the reference program's by a relative error of at most 0.012.
Values may be sent and summed in bfloat16 or wider, within the bound.
No kernel may reach another device: no remote copies, remote signals or barrier semaphores. Data moves between devices by JAX's collectives and lax.ppermute only.
A program may use at most 64 MiB of HBM per device.

```python
import jax
import jax.numpy as jnp
from jax import lax

C = 128
B = 8
P_SIZE = 128
NT = 16
HZ = 6
NCX = 4
NCY = 8


def place_ends(result, rng, smallest, top_value):
    index_at = [jax.random.randint(jax.random.fold_in(rng, axis), (), 0, length) for axis, length in enumerate(result.shape)]
    main_axis = result.shape.index(max(result.shape))
    beside = index_at[:main_axis] + [(index_at[main_axis] + 1) % result.shape[main_axis]] + index_at[main_axis + 1:]
    return result.at[tuple(index_at)].set(smallest).at[tuple(beside)].set(top_value)


def block_scale(own_key, extent, shards, low, high):
    level = 1.0
    for position, blocks in shards:
        draws = jax.random.uniform(jax.random.fold_in(jax.random.fold_in(own_key, 6), position), (blocks,), jnp.float32, low / len(shards), high / len(shards))
        level = level * jnp.repeat(jnp.exp(draws), extent[position] // blocks).reshape((-1,) + (1,) * (len(extent) - 1 - position))
    return level


def scatter_about(rng, extent, deviation, limit, pieces=(), held_as=jnp.bfloat16):
    gain = block_scale(rng, extent, pieces, -0.22, 0.18) if pieces else 1.0
    drawn = jax.random.normal(rng, extent, jnp.float32) * deviation * gain
    return jnp.minimum(jnp.maximum(drawn, -limit), limit).astype(held_as)


def setup_inputs(seed: int = 0, part: int = 0) -> dict:
    key_list = jax.random.split(jax.random.key(seed), 10)
    part_keys = jax.random.split(jax.random.fold_in(key_list[9], part), 10)
    features = scatter_about(part_keys[0], (NCX, NCY, P_SIZE, C), 1.0, 6.0, ((0, 4), (1, 4)))
    positions = jnp.clip(1.0 * jax.random.uniform(part_keys[1], (NCX, NCY, 3, P_SIZE), jnp.float32) ** block_scale(part_keys[1], (NCX, NCY, 3, P_SIZE), ((0, 4), (1, 4)), -0.2, 0.2), 0.0, 1.0)
    bead_types = place_ends(jax.random.randint(part_keys[2], (NCX, NCY, P_SIZE), 0, NT), jax.random.fold_in(part_keys[2], 1), 0, NT - 1).astype(jnp.int32)
    cell_counts = place_ends(jax.random.randint(part_keys[3], (NCX, NCY), P_SIZE * 3 // 8, P_SIZE + 1), jax.random.fold_in(part_keys[3], 1), P_SIZE * 3 // 8, P_SIZE).astype(jnp.int32)
    w_value = scatter_about(key_list[4], (C, C), C ** -0.5, 0.5)
    w_radial = scatter_about(key_list[5], (B, C), 0.1, 0.6, (), jnp.float32)
    type_gain = jnp.clip(1.0 + 0.18 * jax.random.normal(key_list[6], (NT, C), jnp.float32), 0.1, 1.9)
    w_out = scatter_about(key_list[7], (C, C), C ** -0.5, 0.5)
    cotangent = scatter_about(part_keys[8], (NCX, NCY, P_SIZE, C), 1.0, 6.0, ((0, 4), (1, 4)))
    return {"features": features, "positions": positions, "bead_types": bead_types, "cell_counts": cell_counts, "w_value": w_value, "w_radial": w_radial, "type_gain": type_gain, "w_out": w_out, "cotangent": cotangent}


soften = 0.01
stencil = [(-1, -1), (-1, 0), (-1, 1), (0, -1), (0, 0), (0, 1), (1, -1), (1, 0), (1, 1)]

def pair_terms(pos_own, pos_near, shift_x, shift_y, is_self, basis_count):
    slot_count = pos_own.shape[-1]
    offsets = (float(shift_x), float(shift_y), 0.0)
    scales = (1.0, 1.0, float(HZ))
    deltas = [(pos_near[:, :, component, None, :] - pos_own[:, :, component, :, None]) * scales[component] + offsets[component] for component in range(3)]
    dist_sq = deltas[0] * deltas[0] + deltas[1] * deltas[1] + deltas[2] * deltas[2]
    pair_mask = pos_own[:, :, 3, :, None] * pos_near[:, :, 3, None, :]
    if is_self:
        pair_mask = pair_mask * (1.0 - jnp.eye(slot_count, dtype=jnp.float32))
    radius = jnp.sqrt(dist_sq + soften)
    inside = jnp.maximum(1.0 - dist_sq, 0.0)
    envelope = inside * inside
    centres = jnp.arange(basis_count, dtype=jnp.float32) / (basis_count - 1)
    width_gamma = 0.5 * (basis_count - 1) ** 2
    offset_r = radius[:, :, None] - centres[None, None, :, None, None]
    gaussian = jnp.exp(-width_gamma * offset_r * offset_r)
    weights = ((pair_mask * envelope)[:, :, None] * gaussian).astype(jnp.bfloat16)
    slope_r2 = pair_mask[:, :, None] * gaussian * (-2.0 * inside[:, :, None] - envelope[:, :, None] * width_gamma * offset_r / radius[:, :, None])
    scaled_deltas = [deltas[component] * scales[component] for component in range(3)]
    return (weights, slope_r2, scaled_deltas)

def reference(features, positions, bead_types, cell_counts, w_value, w_radial, type_gain, w_out, cotangent):
    cells_x, cells_y, slot_count, channels = features.shape
    basis_count = w_radial.shape[0]
    valid_slot = (jnp.arange(slot_count, dtype=jnp.int32)[None, None, :] < cell_counts[:, :, None]).astype(jnp.float32)
    pos_valid = jnp.concatenate([positions, valid_slot[:, :, None, :]], axis=2)
    flat_feat = features.reshape(-1, channels)
    projected = jnp.dot(flat_feat, w_value, preferred_element_type=jnp.float32)
    onehot = (bead_types.reshape(-1)[:, None] == jnp.arange(type_gain.shape[0], dtype=jnp.int32)[None, :]).astype(jnp.float32)
    bead_gain = jnp.dot(onehot, type_gain, precision=lax.Precision.HIGHEST)
    carried = (projected * bead_gain).astype(jnp.bfloat16).reshape(cells_x, cells_y, slot_count, channels)
    summed = jnp.zeros((cells_x, cells_y, basis_count, slot_count, channels), jnp.float32)
    for shift_x, shift_y in stencil:
        near_pos = jnp.roll(pos_valid, (-shift_x, -shift_y), axis=(0, 1))
        near_val = jnp.roll(carried, (-shift_x, -shift_y), axis=(0, 1))
        weights, slope_r2, deltas = pair_terms(pos_valid, near_pos, shift_x, shift_y, shift_x == 0 and shift_y == 0, basis_count)
        summed = summed + jnp.einsum('abkij,abjc->abkic', weights.astype(jnp.float32), near_val.astype(jnp.float32))
    aggregate = lax.optimization_barrier(jnp.sum(summed * w_radial[None, None, :, None, :], axis=2))
    agg_half = aggregate.astype(jnp.bfloat16).reshape(-1, channels)
    pre_act = jnp.dot(agg_half, w_out, preferred_element_type=jnp.float32)
    sigmoid_act = jax.nn.sigmoid(pre_act)
    out_feat = (flat_feat.astype(jnp.float32) + pre_act * sigmoid_act).astype(jnp.bfloat16)
    grad_pre = (cotangent.reshape(-1, channels).astype(jnp.float32) * sigmoid_act * (1.0 + pre_act * (1.0 - sigmoid_act))).astype(jnp.bfloat16)
    grad_wout = jnp.dot(agg_half.T, grad_pre, preferred_element_type=jnp.float32)
    grad_agg = jnp.dot(grad_pre, w_out.T, preferred_element_type=jnp.float32).astype(jnp.bfloat16).reshape(cells_x, cells_y, slot_count, channels)
    grad_wradial = lax.optimization_barrier(jnp.sum(summed * grad_agg.astype(jnp.float32)[:, :, None], axis=(0, 1, 3)))
    scaled = (grad_agg.astype(jnp.float32)[:, :, None] * w_radial[None, None, :, None, :]).astype(jnp.bfloat16)
    grad_carried = jnp.zeros((cells_x, cells_y, slot_count, channels), jnp.float32)
    grad_pos = jnp.zeros((cells_x, cells_y, 3, slot_count), jnp.float32)
    for shift_x, shift_y in stencil:
        near_pos = jnp.roll(pos_valid, (-shift_x, -shift_y), axis=(0, 1))
        near_val = jnp.roll(carried, (-shift_x, -shift_y), axis=(0, 1))
        weights, slope_r2, deltas = pair_terms(pos_valid, near_pos, shift_x, shift_y, shift_x == 0 and shift_y == 0, basis_count)
        weight_grad = jnp.einsum('abkic,abjc->abkij', scaled.astype(jnp.float32), near_val.astype(jnp.float32))
        pair_pull = lax.optimization_barrier(jnp.sum(weight_grad * slope_r2, axis=2))
        own_pull = jnp.stack([-2.0 * lax.optimization_barrier(jnp.sum(pair_pull * delta_one, axis=3)) for delta_one in deltas], axis=2)
        far_pull = jnp.stack([2.0 * lax.optimization_barrier(jnp.sum(pair_pull * delta_one, axis=2)) for delta_one in deltas], axis=2)
        far_value = jnp.einsum('abkij,abkic->abjc', weights.astype(jnp.float32), scaled.astype(jnp.float32))
        grad_pos = grad_pos + own_pull + jnp.roll(far_pull, (shift_x, shift_y), axis=(0, 1))
        grad_carried = grad_carried + jnp.roll(far_value, (shift_x, shift_y), axis=(0, 1))
    flat_carried = grad_carried.reshape(-1, channels)
    grad_half = (flat_carried * bead_gain).astype(jnp.bfloat16)
    grad_feat = (cotangent.reshape(-1, channels).astype(jnp.float32) + jnp.dot(grad_half, w_value.T, preferred_element_type=jnp.float32)).astype(jnp.bfloat16)
    grad_wvalue = jnp.dot(flat_feat.T, grad_half, preferred_element_type=jnp.float32)
    grad_gain = jnp.dot(onehot.T, flat_carried * projected, precision=lax.Precision.HIGHEST)
    return (out_feat.reshape(cells_x, cells_y, slot_count, channels), grad_feat.reshape(cells_x, cells_y, slot_count, channels), grad_pos, grad_wvalue, grad_wradial, grad_gain, grad_wout)
```

```python
import functools
import math

import jax
import jax.numpy as jnp
from jax import lax
from jax.experimental import pallas as pl
from jax.experimental.pallas import tpu as pltpu
from jax.sharding import PartitionSpec as P

HZ = 6
SOFTEN = 0.01
FAR = 1024.0
AUX = 16
STRIP = 32
LANES = 128


f32 = jnp.float32
bf16 = jnp.bfloat16


def split3(x):
    hi = x.astype(bf16)
    rest = x - hi.astype(f32)
    mid = rest.astype(bf16)
    low = (rest - mid.astype(f32)).astype(bf16)
    return hi, mid, low


def dot(a, b):
    return jnp.dot(a, b, preferred_element_type=f32)


def dot_t(a, b):
    return lax.dot_general(a, b, (((1,), (1,)), ((), ())), preferred_element_type=f32)


def bead_onehot_t(types_row, type_count, slots):
    rows = lax.broadcasted_iota(jnp.int32, (slots, slots), 0)
    hit = (rows == types_row) | (rows == types_row + type_count) | (rows == types_row + 2 * type_count)
    return jnp.where(hit, 1.0, 0.0).astype(f32)


def gains_of(types_row, gain_ref, gain_rows, slots):
    type_count = gain_ref.shape[0]
    hi, mid, low = split3(gain_ref[...])
    gain_rows[...] = jnp.zeros_like(gain_rows)
    gain_rows[0:type_count, :] = hi.astype(f32)
    gain_rows[type_count : 2 * type_count, :] = mid.astype(f32)
    gain_rows[2 * type_count : 3 * type_count, :] = low.astype(f32)
    onehot_t = bead_onehot_t(types_row, type_count, slots)
    return onehot_t, dot(onehot_t.T.astype(bf16), gain_rows[...].astype(bf16))


def pack_kernel(order, counts, feat, pos, types, w_value, type_gain, packed, gain_rows):
    slots = feat.shape[2]
    for place in range(2):
        cell = jnp.where(order[1] == 0, place, 1 - place)
        projected = dot(feat[0, cell], w_value[...])
        _, gain = gains_of(types[0, pl.ds(cell, 1), :], type_gain, gain_rows, slots)
        packed[place, 0:slots, :] = (projected * gain).astype(bf16)
        lane = lax.broadcasted_iota(jnp.int32, (1, slots), 1)
        valid = lane < counts[0, cell]
        parts = [[], [], []]
        for comp in range(3):
            row = pos[0, cell, comp : comp + 1, :]
            if comp == 2:
                row = row * float(HZ)
            row = jnp.where(valid, row, -FAR)
            for which, part in enumerate(split3(row)):
                parts[which].append(part.astype(f32))
        rows = parts[0] + parts[1] + parts[2]
        rows.append(jnp.zeros((AUX - len(rows), slots), f32))
        packed[place, slots : slots + AUX, :] = jnp.concatenate(rows, axis=0).astype(bf16)


def near_positions(ref, cell, slots):
    aux = ref[cell, slots : slots + AUX, :].astype(f32)
    return aux[0:3] + aux[3:6] + aux[6:9]


def load_near(order, refs, slots, near_pos):
    own, row_a, row_b, col_a, col_b = refs
    sx = jnp.where(order[0] == 0, 1.0, -1.0).astype(f32)
    sy = jnp.where(order[1] == 0, 1.0, -1.0).astype(f32)
    cells = []
    for col in range(4):
        for row in range(3):
            if col == 0:
                cells.append((col_b, row))
            elif col == 3:
                cells.append((col_a, row))
            else:
                cells.append(((row_a, own, row_b)[row], col - 1))
    for index, (ref, cell) in enumerate(cells):
        col, row = index // 3, index % 3
        xyz = near_positions(ref, cell, slots)
        shift_x = sx * float(1 - row)
        shift_y = sy * float(col)
        near_pos[index, 0:1, :] = xyz[0:1] + shift_x
        near_pos[index, 1:2, :] = xyz[1:2] + shift_y
        near_pos[index, 2:3, :] = xyz[2:3]
    return cells


def own_columns(near_pos, own_pos, slots):
    for place in range(2):
        index = (place + 1) * 3 + 1
        xyz = near_pos[index, 0:3, :]
        unused = xyz[0:1] < -0.5 * FAR
        for comp in range(3):
            row = jnp.where(unused, FAR, xyz[comp : comp + 1])
            own_pos[place, comp] = jnp.broadcast_to(row, (slots, slots)).T


def pair_terms(near_pos, index, own_xyz, is_self, first_row, basis_count):
    n1 = float(basis_count - 1)
    delta = [near_pos[index, comp : comp + 1, :] - own_xyz[comp] for comp in range(3)]
    dist_sq = delta[0] * delta[0] + delta[1] * delta[1] + delta[2] * delta[2]
    dist_sq = jnp.minimum(dist_sq, 1.0)
    inside = 1.0 - dist_sq
    radius_sq = dist_sq + SOFTEN
    inverse = lax.rsqrt(radius_sq)
    radius = radius_sq * inverse
    gauss = jnp.exp(radius_sq * (-0.5 * n1 * n1))
    step = jnp.exp(radius * n1)
    if is_self:
        rows = first_row + lax.broadcasted_iota(jnp.int32, gauss.shape, 0)
        lanes = lax.broadcasted_iota(jnp.int32, gauss.shape, 1)
        gauss = jnp.where(rows == lanes, 0.0, gauss)
    return delta, inside, inverse, gauss, step


def forward_kernel(
    basis_count, order, own, row_a, row_b, col_a, col_b, feat, cotangent, w_radial, w_out,
    out_feat, grad_agg, grad_wout, grad_wradial,
    near_pos, own_pos, near_val, weights,
):
    slots = feat.shape[2]
    cells = load_near(order, (own, row_a, row_b, col_a, col_b), slots, near_pos)
    own_columns(near_pos, own_pos, slots)
    for index, (ref, cell) in enumerate(cells):
        near_val[index * slots : (index + 1) * slots, :] = ref[cell, 0:slots, :]
    span = 9 * slots
    for place in range(2):

        def strip(s, carry, place=place):
            first = pl.multiple_of(s * STRIP, STRIP)
            own_xyz = [own_pos[place, comp, pl.ds(first, STRIP), :] for comp in range(3)]
            for block in range(9):
                index = place * 3 + block
                _, inside, _, gauss, step = pair_terms(
                    near_pos, index, own_xyz, block == 4, first, basis_count
                )
                weight = inside * inside * gauss
                for k in range(basis_count):
                    weights[k, pl.ds(first, STRIP), block * slots : (block + 1) * slots] = (
                        weight.astype(bf16)
                    )
                    if k < basis_count - 1:
                        weight = weight * step
            return carry

        lax.fori_loop(0, slots // STRIP, strip, 0)
        values = near_val[place * 3 * slots : place * 3 * slots + span, :]
        summed = [dot(weights[k], values) for k in range(basis_count)]
        scale = [math.exp(-0.5 * k * k) for k in range(basis_count)]
        radial = [w_radial[k : k + 1, :] * scale[k] for k in range(basis_count)]
        aggregate = summed[0] * radial[0]
        for k in range(1, basis_count):
            aggregate = aggregate + summed[k] * radial[k]
        agg_half = aggregate.astype(bf16)
        cell = jnp.where(order[1] == 0, place, 1 - place)
        pre_act = dot(agg_half, w_out[...])
        sig = jax.nn.sigmoid(pre_act)
        out_feat[0, cell] = (feat[0, cell].astype(f32) + pre_act * sig).astype(bf16)
        grad_pre = (
            cotangent[0, cell].astype(f32) * sig * (1.0 + pre_act * (1.0 - sig))
        ).astype(bf16)
        agg = dot_t(grad_pre, w_out[...]).astype(bf16)
        grad_agg[place] = agg
        agg = agg.astype(f32)
        wout = dot(aggregate.T.astype(bf16), grad_pre)
        wradial = jnp.concatenate(
            [jnp.sum(agg * summed[k], axis=0, keepdims=True) * scale[k] for k in range(basis_count)],
            axis=0,
        )
        if place == 0:
            grad_wout[...] = wout
            grad_wradial[...] = wradial
        else:
            grad_wout[...] += wout
            grad_wradial[...] += wradial


def backward_kernel(
    basis_count, order, own, row_a, row_b, col_a, col_b,
    g_own, g_row_a, g_row_b, g_col_a, g_col_b,
    feat, types, cotangent, w_value, w_radial, type_gain, grad_wout, grad_wradial,
    grad_feat, grad_pos, payload,
    near_pos, own_pos, near_both, weights, own_both, weight_grad, pull_acc, gain_rows,
):
    slots, channels = feat.shape[2], feat.shape[3]
    n1 = float(basis_count - 1)
    gamma = 0.5 * n1 * n1
    cells = load_near(order, (own, row_a, row_b, col_a, col_b), slots, near_pos)
    own_columns(near_pos, own_pos, slots)
    g_refs = {id(own): g_own, id(row_a): g_row_a, id(row_b): g_row_b, id(col_a): g_col_a, id(col_b): g_col_b}
    for index, (ref, cell) in enumerate(cells):
        here = slice(index * slots, (index + 1) * slots)
        near_both[here, 0:channels] = ref[cell, 0:slots, :]
        near_both[here, channels : 2 * channels] = g_refs[id(ref)][cell]
    radial = [w_radial[k : k + 1, :] * math.exp(-0.5 * k * k) for k in range(basis_count)]
    span = 9 * slots
    type_count = type_gain.shape[0]
    wvalue = None
    for place in range(2):
        carried = own[place, 0:slots, :].astype(f32)
        agg = g_own[place].astype(f32)
        for k in range(basis_count):
            own_both[k, :, 0:channels] = (agg * radial[k]).astype(bf16)
            own_both[k, :, channels : 2 * channels] = (carried * radial[k]).astype(bf16)
        near = slice(place * 3 * slots, place * 3 * slots + span)
        for k in range(basis_count):
            weight_grad[k] = dot_t(own_both[k], near_both[near, :])

        def strip(s, carry, place=place):
            first = pl.multiple_of(s * STRIP, STRIP)
            own_xyz = [own_pos[place, comp, pl.ds(first, STRIP), :] for comp in range(3)]
            total = [jnp.zeros((STRIP, slots), f32) for _ in range(3)]
            for block in range(9):
                index = place * 3 + block
                there = slice(block * slots, (block + 1) * slots)
                delta, inside, inverse, gauss, step = pair_terms(
                    near_pos, index, own_xyz, block == 4, first, basis_count
                )
                envelope = inside * inside
                weight = envelope * gauss
                for k in range(basis_count):
                    weights[k, pl.ds(first, STRIP), there] = weight.astype(bf16)
                    if k < basis_count - 1:
                        weight = weight * step
                value = weight_grad[basis_count - 1, pl.ds(first, STRIP), there]
                slope = None
                for k in range(basis_count - 2, -1, -1):
                    slope = value if slope is None else value + step * slope
                    value = weight_grad[k, pl.ds(first, STRIP), there] + step * value
                pull = gauss * (
                    envelope * ((gamma / n1) * inverse * step * slope - gamma * value)
                    - 2.0 * inside * value
                )
                for comp in range(3):
                    total[comp] = total[comp] + pull * delta[comp]
            for comp in range(3):
                pull_acc[comp, pl.ds(first, STRIP), :] = total[comp]
            return carry

        lax.fori_loop(0, slots // STRIP, strip, 0)
        cell = jnp.where(order[1] == 0, place, 1 - place)
        rows = []
        for comp in range(3):
            row = jnp.sum(pull_acc[comp].T, axis=0, keepdims=True)
            rows.append(row * (-2.0 * HZ if comp == 2 else -2.0))
        grad_pos[0, cell] = jnp.concatenate(rows, axis=0)
        values = near_both[near, channels : 2 * channels]
        carried_grad = dot(weights[0], values) * radial[0]
        for k in range(1, basis_count):
            carried_grad = carried_grad + dot(weights[k], values) * radial[k]
        here = feat[0, cell]
        projected = dot(here, w_value[...])
        onehot_t, gain = gains_of(types[0, pl.ds(cell, 1), :], type_gain, gain_rows, slots)
        half = (carried_grad * gain).astype(bf16)
        grad_feat[0, cell] = (
            cotangent[0, cell].astype(f32) + dot_t(half, w_value[...])
        ).astype(bf16)
        value_part = dot(here.astype(f32).T.astype(bf16), half)
        hi, mid, _ = split3(carried_grad * projected)
        select = onehot_t[0:type_count].astype(bf16)
        gain_part = dot(select, hi) + dot(select, mid)
        if place == 0:
            wvalue, ggain = value_part, gain_part
        else:
            wvalue, ggain = wvalue + value_part, ggain + gain_part
    payload[0:channels, :] = wvalue.astype(bf16)
    payload[channels : 2 * channels, :] = grad_wout[...].astype(bf16)
    tail = jnp.concatenate([ggain, grad_wradial[...]], axis=0)
    pad = payload.shape[0] - 2 * channels - tail.shape[0]
    if pad:
        tail = jnp.concatenate([tail, jnp.zeros((pad, channels), f32)], axis=0)
    payload[2 * channels :, :] = tail.astype(bf16)


def pair_routes(axis):
    count = lax.axis_size(axis)
    assert count % 2 == 0 and count > 2
    even = [(i, i ^ 1) for i in range(count)]
    odd = [(i, (i + 1) % count if i % 2 else (i - 1) % count) for i in range(count)]
    return even, odd


def exchange(to_even, to_odd, axis):
    even, odd = pair_routes(axis)
    from_odd = lax.ppermute(to_odd, axis, odd)
    from_even = lax.ppermute(to_even, axis, even)
    return from_even, from_odd


def halo(own):
    row_a, row_b = exchange(own, own, "gx")
    send_a = jnp.stack([row_a[1], own[1], row_b[1]])
    send_b = jnp.stack([row_a[0], own[0], row_b[0]])
    col_a, col_b = exchange(send_a, send_b, "gy")
    return own, row_a, row_b, col_a, col_b


def reduce_over(part, axis, wide):
    count = lax.axis_size(axis)
    assert count & (count - 1) == 0
    step = 1
    total = part.astype(f32)
    while step < count:
        if wide and step * 4 <= count:
            got = [
                lax.ppermute(part, axis, [(i, i ^ (step * m)) for i in range(count)]).astype(f32)
                for m in (1, 2, 3)
            ]
            total = (part.astype(f32) + got[0]) + (got[1] + got[2])
            step *= 4
        else:
            got = lax.ppermute(part, axis, [(i, i ^ step) for i in range(count)])
            total = part.astype(f32) + got.astype(f32)
            step *= 2
        part = total.astype(bf16)
    return total, part


def on_device(
    features, positions, bead_types, cell_counts, w_value, w_radial, type_gain, w_out, cotangent
):
    row_count, col_count, slots, channels = features.shape
    basis_count, type_count = w_radial.shape[0], type_gain.shape[0]
    assert row_count == 1 and col_count == 2 and slots == channels == LANES
    assert 3 * type_count <= slots and type_count % 8 == 0 and basis_count % 8 == 0
    order = jnp.stack([lax.axis_index("gx") % 2, lax.axis_index("gy") % 2]).astype(jnp.int32)
    smem = pl.BlockSpec(memory_space=pltpu.SMEM)
    vmem = pl.BlockSpec(memory_space=pltpu.VMEM)
    params = pltpu.CompilerParams(vmem_limit_bytes=56 * 2**20)
    packed = pl.pallas_call(
        pack_kernel,
        out_shape=jax.ShapeDtypeStruct((2, slots + AUX, channels), bf16),
        in_specs=[smem, smem] + [vmem] * 5,
        out_specs=vmem,
        scratch_shapes=[pltpu.VMEM((slots, channels), f32)],
        compiler_params=params,
        name="pack",
    )(order, cell_counts, features, positions, bead_types, w_value, type_gain)
    near = halo(packed)
    geometry = [pltpu.VMEM((12, 8, slots), f32), pltpu.VMEM((2, 3, slots, slots), f32)]
    out_feat, grad_agg, grad_wout, grad_wradial = pl.pallas_call(
        functools.partial(forward_kernel, basis_count),
        out_shape=(
            jax.ShapeDtypeStruct(features.shape, bf16),
            jax.ShapeDtypeStruct((2, slots, channels), bf16),
            jax.ShapeDtypeStruct((channels, channels), f32),
            jax.ShapeDtypeStruct((basis_count, channels), f32),
        ),
        in_specs=[smem] + [vmem] * 9,
        out_specs=(vmem,) * 4,
        scratch_shapes=geometry
        + [
            pltpu.VMEM((12 * slots, channels), bf16),
            pltpu.VMEM((basis_count, slots, 9 * slots), bf16),
        ],
        compiler_params=params,
        name="forward",
    )(order, *near, features, cotangent, w_radial, w_out)
    near_agg = halo(grad_agg)
    rows = 2 * channels + type_count + basis_count
    rows = -(-rows // 16) * 16
    grad_feat, grad_pos, part = pl.pallas_call(
        functools.partial(backward_kernel, basis_count),
        out_shape=(
            jax.ShapeDtypeStruct(features.shape, bf16),
            jax.ShapeDtypeStruct(positions.shape, f32),
            jax.ShapeDtypeStruct((rows, channels), bf16),
        ),
        in_specs=[smem] + [vmem] * 18,
        out_specs=(vmem,) * 3,
        scratch_shapes=geometry
        + [
            pltpu.VMEM((12 * slots, 2 * channels), bf16),
            pltpu.VMEM((basis_count, slots, 9 * slots), bf16),
            pltpu.VMEM((basis_count, slots, 2 * channels), bf16),
            pltpu.VMEM((basis_count, slots, 9 * slots), f32),
            pltpu.VMEM((3, slots, slots), f32),
            pltpu.VMEM((slots, channels), f32),
        ],
        compiler_params=params,
        name="backward",
    )(
        order, *near, *near_agg, features, bead_types, cotangent, w_value, w_radial, type_gain,
        grad_wout, grad_wradial,
    )
    _, part = reduce_over(part, "gx", True)
    total, _ = reduce_over(part, "gy", False)
    tail = 2 * channels
    return (
        out_feat,
        grad_feat,
        grad_pos,
        total[:channels],
        total[tail + type_count : tail + type_count + basis_count],
        total[tail : tail + type_count],
        total[channels:tail],
    )


def solution(mesh):
    cell = P(("frame", "gx"), "gy", None, None)
    return jax.shard_map(
        on_device,
        mesh=mesh,
        in_specs=(
            cell, cell, P(("frame", "gx"), "gy", None), P(("frame", "gx"), "gy"),
            P(), P(), P(), P(), cell,
        ),
        out_specs=(cell, cell, cell) + (P("frame", None),) * 4,
        check_vma=False,
    )
```

```python
import functools
import math

import jax
import jax.numpy as jnp
from jax import lax
from jax.experimental import pallas as pl
from jax.experimental.pallas import tpu as pltpu
from jax.sharding import PartitionSpec as P

HZ = 6
SOFTEN = 0.01
FAR = 1024.0
AUX = 16
STRIP = 32
LANES = 128


f32 = jnp.float32
bf16 = jnp.bfloat16


def split3(x):
    hi = x.astype(bf16)
    rest = x - hi.astype(f32)
    mid = rest.astype(bf16)
    low = (rest - mid.astype(f32)).astype(bf16)
    return hi, mid, low


def dot(a, b):
    return jnp.dot(a, b, preferred_element_type=f32)


def dot_t(a, b):
    return lax.dot_general(a, b, (((1,), (1,)), ((), ())), preferred_element_type=f32)


def identity(size):
    rows = lax.broadcasted_iota(jnp.int32, (size, size), 0)
    lanes = lax.broadcasted_iota(jnp.int32, (size, size), 1)
    return jnp.where(rows == lanes, 1.0, 0.0).astype(bf16)


def gain_columns(type_gain):
    parts = [part.astype(f32) for part in split3(type_gain[...])]
    count, channels = type_gain.shape
    rows = jnp.concatenate(parts + [jnp.zeros((channels - 3 * count, channels), f32)], axis=0)
    return rows.T.astype(bf16)


def onehot_rows(types_row, type_count, slots):
    rows = lax.broadcasted_iota(jnp.int32, (slots, slots), 0)
    hit = (rows == types_row) | (rows == types_row + type_count) | (rows == types_row + 2 * type_count)
    return jnp.where(hit, 1.0, 0.0).astype(bf16)


def pack_kernel(order, counts, feat, pos, types, packed):
    slots = feat.shape[2]
    for place in range(2):
        cell = jnp.where(order[1] == 0, place, 1 - place)
        packed[place, 0:slots, :] = feat[0, cell]
        lane = lax.broadcasted_iota(jnp.int32, (1, slots), 1)
        valid = lane < counts[0, cell]
        parts = [[], [], []]
        for comp in range(3):
            row = pos[0, cell, comp : comp + 1, :]
            if comp == 2:
                row = row * float(HZ)
            row = jnp.where(valid, row, -FAR)
            for which, part in enumerate(split3(row)):
                parts[which].append(part.astype(f32))
        rows = parts[0] + parts[1] + parts[2]
        rows.append(types[0, pl.ds(cell, 1), :].astype(f32))
        rows.append(jnp.zeros((AUX - len(rows), slots), f32))
        packed[place, slots : slots + AUX, :] = jnp.concatenate(rows, axis=0).astype(bf16)


def pair_terms(near_pos, index, own_xyz, is_self, first_row, basis_count):
    n1 = float(basis_count - 1)
    gamma = 0.5 * n1 * n1
    delta = [near_pos[index, comp : comp + 1, :] - own_xyz[comp] for comp in range(3)]
    dist_sq = delta[0] * delta[0] + delta[1] * delta[1] + delta[2] * delta[2]
    dist_sq = jnp.minimum(dist_sq, 1.0)
    inside = 1.0 - dist_sq
    radius_sq = dist_sq + SOFTEN
    inverse = lax.rsqrt(radius_sq)
    radius = radius_sq * inverse
    gauss = jnp.exp(radius_sq * -gamma)
    step = jnp.exp(radius * n1)
    if is_self:
        rows = first_row + lax.broadcasted_iota(jnp.int32, gauss.shape, 0)
        lanes = lax.broadcasted_iota(jnp.int32, gauss.shape, 1)
        gauss = jnp.where(rows == lanes, 0.0, gauss)
    weight = inside * inside * gauss
    value_factor = -2.0 * (inside * gauss) - gamma * weight
    slope_factor = (gamma / n1) * weight * (inverse * step)
    return step, weight, value_factor, slope_factor


def main_kernel(
    basis_count, order, own, row_a, row_b, cotangent, w_value, w_radial, type_gain, w_out,
    out_feat, pay_a, pay_b, part, own_acc,
    near_pos, own_pos, near_feat, near_val, onehot, projected, gains, weights, steps, values, slopes,
    summed, scaled, weight_grad, grad_val, pull_own, pull_far,
):
    slots, channels = cotangent.shape[2], cotangent.shape[3]
    type_count = type_gain.shape[0]
    span = 9 * slots
    eye = identity(slots)
    sx = jnp.where(order[0] == 0, 1.0, -1.0).astype(f32)
    sy = jnp.where(order[1] == 0, 1.0, -1.0).astype(f32)
    for index in range(12):
        col, row = index // 3, index % 3
        ref = (row_a, own, row_b)[row]
        here = slice(index * slots, (index + 1) * slots)
        near_feat[here, :] = ref[col, 0:slots, :]
        aux = ref[col, slots : slots + AUX, :].astype(f32)
        xyz = aux[0:3] + aux[3:6] + aux[6:9]
        near_pos[index, 0:1, :] = xyz[0:1] + sx * float(1 - row)
        near_pos[index, 1:2, :] = xyz[1:2] + sy * float(col)
        near_pos[index, 2:3, :] = xyz[2:3]
        onehot[:, here] = onehot_rows(aux[9:10].astype(jnp.int32), type_count, slots)
        if row == 1 and col in (1, 2):
            unused = xyz[0:1] < -0.5 * FAR
            for comp in range(3):
                line = jnp.where(unused, FAR, near_pos[index, comp : comp + 1, :])
                own_pos[col - 1, comp] = jnp.broadcast_to(line, (slots, slots)).T
    projected[...] = dot_t(w_value[...].astype(f32).T.astype(bf16), near_feat[...])
    gains[...] = dot(gain_columns(type_gain), onehot[...])
    for index in range(12):
        here = slice(index * slots, (index + 1) * slots)
        carried_t = (projected[:, here] * gains[:, here]).astype(bf16)
        near_val[here, :] = dot_t(eye, carried_t).astype(bf16)
    scale = [math.exp(-0.5 * k * k) for k in range(basis_count)]
    radial = [w_radial[k : k + 1, :] * scale[k] for k in range(basis_count)]
    wout = wradial = None
    for place in range(2):
        near = slice(place * 3 * slots, place * 3 * slots + span)

        def pairs(s, carry, place=place):
            first = pl.multiple_of(s * STRIP, STRIP)
            strip = pl.ds(first, STRIP)
            own_xyz = [own_pos[place, comp, strip, :] for comp in range(3)]
            for block in range(9):
                there = slice(block * slots, (block + 1) * slots)
                step, weight, value_factor, slope_factor = pair_terms(
                    near_pos, place * 3 + block, own_xyz, block == 4, first, basis_count
                )
                steps[strip, there] = step
                values[strip, there] = value_factor
                slopes[strip, there] = slope_factor
                for k in range(basis_count):
                    weights[k, strip, there] = weight.astype(bf16)
                    if k < basis_count - 1:
                        weight = weight * step
            return carry

        lax.fori_loop(0, slots // STRIP, pairs, 0)
        aggregate = None
        for k in range(basis_count):
            summed[k] = dot(weights[k], near_val[near, :])
            term = summed[k] * radial[k]
            aggregate = term if aggregate is None else aggregate + term
        agg_half = aggregate.astype(bf16)
        cell = jnp.where(order[1] == 0, place, 1 - place)
        pre_act = dot(agg_half, w_out[...])
        sig = jax.nn.sigmoid(pre_act)
        center = near_feat[((place + 1) * 3 + 1) * slots : ((place + 1) * 3 + 2) * slots, :]
        out_feat[0, cell] = (center.astype(f32) + pre_act * sig).astype(bf16)
        grad_pre = (
            cotangent[0, cell].astype(f32) * sig * (1.0 + pre_act * (1.0 - sig))
        ).astype(bf16)
        agg = dot_t(grad_pre, w_out[...]).astype(bf16).astype(f32)
        wout_part = dot(aggregate.T.astype(bf16), grad_pre)
        rows = []
        for k in range(basis_count):
            rows.append(jnp.sum(agg * summed[k], axis=0, keepdims=True) * scale[k])
            scaled[k] = (agg * radial[k]).astype(bf16)
        wradial_part = jnp.concatenate(rows, axis=0)
        wout = wout_part if wout is None else wout + wout_part
        wradial = wradial_part if wradial is None else wradial + wradial_part
        for k in range(basis_count):
            weight_grad[k] = dot_t(scaled[k], near_val[near, :])

        pull_far[...] = jnp.zeros_like(pull_far) if place == 0 else pull_far[...]

        def pulls(s, carry, place=place):
            first = pl.multiple_of(s * STRIP, STRIP)
            strip = pl.ds(first, STRIP)
            own_xyz = [own_pos[place, comp, strip, :] for comp in range(3)]
            total = [jnp.zeros((STRIP, slots), f32) for _ in range(3)]
            for block in range(9):
                index = place * 3 + block
                there = slice(block * slots, (block + 1) * slots)
                step = steps[strip, there]
                value = weight_grad[basis_count - 1, strip, there]
                slope = None
                for k in range(basis_count - 2, -1, -1):
                    slope = value if slope is None else value + step * slope
                    value = weight_grad[k, strip, there] + step * value
                pull = values[strip, there] * value + slopes[strip, there] * slope
                for comp in range(3):
                    force = pull * (near_pos[index, comp : comp + 1, :] - own_xyz[comp])
                    total[comp] = total[comp] + force
                    pull_far[index, comp] += (force[0:8] + force[8:16]) + (force[16:24] + force[24:32])
            for comp in range(3):
                pull_own[place, comp, strip, :] = total[comp]
            return carry

        lax.fori_loop(0, slots // STRIP, pulls, 0)
        scaled_t = [dot_t(eye, scaled[k]).astype(bf16) for k in range(basis_count)]
        part_t = dot(scaled_t[0], weights[0])
        for k in range(1, basis_count):
            part_t = part_t + dot(scaled_t[k], weights[k])
        if place == 0:
            grad_val[:, near] = part_t
            grad_val[:, place * 3 * slots + span :] = jnp.zeros((channels, 12 * slots - span), f32)
        else:
            grad_val[:, near] += part_t
    half = (grad_val[...] * gains[...]).astype(bf16)
    wvalue = dot(half, near_feat[...]).T
    hi, mid, _ = split3(grad_val[...] * projected[...])
    ggain = (dot_t(hi, onehot[...]) + dot_t(mid, onehot[...])).T[0:type_count]
    pad = part.shape[0] - 2 * channels - type_count - basis_count
    tail = [ggain, wradial] + ([jnp.zeros((pad, channels), f32)] if pad else [])
    tail = jnp.concatenate(tail, axis=0).astype(bf16)
    for ref in (part, pay_a, pay_b):
        ref[0:channels, :] = wvalue.astype(bf16)
        ref[channels : 2 * channels, :] = wout.astype(bf16)
        ref[2 * channels : part.shape[0], :] = tail
    for index in range(12):
        col, row = index // 3, index % 3
        here = slice(index * slots, (index + 1) * slots)
        lines = []
        for comp in range(3):
            line = jnp.sum(pull_far[index, comp], axis=0, keepdims=True)
            if row == 1 and col in (1, 2):
                line = line - jnp.sum(pull_own[col - 1, comp].T, axis=0, keepdims=True)
            lines.append(line * (2.0 * HZ if comp == 2 else 2.0))
        lines.append(jnp.zeros((AUX - 3, slots), f32))
        lines = jnp.concatenate(lines, axis=0)
        if row == 1:
            own_acc[col, 0:slots, :] = grad_val[:, here]
            own_acc[col, slots : slots + AUX, :] = lines
        else:
            ref = pay_a if row == 0 else pay_b
            base = part.shape[0] + col * (slots + AUX)
            ref[base : base + slots, :] = grad_val[:, here].astype(bf16)
            ref[base + slots : base + slots + AUX, :] = lines.astype(bf16)


def final_kernel(
    tail_rows, order, feat_acc, last_own, last_got, types, cotangent, w_value, type_gain,
    grad_feat, grad_pos, wvalue, wradial, ggain, wout,
):
    slots, channels = cotangent.shape[2], cotangent.shape[3]
    type_count, basis_count = ggain.shape[0], wradial.shape[0]
    total = last_own[0:tail_rows, :].astype(f32) + last_got[0:tail_rows, :].astype(f32)
    wvalue[...] = total[0:channels]
    wout[...] = total[channels : 2 * channels]
    ggain[...] = total[2 * channels : 2 * channels + type_count]
    wradial[...] = total[2 * channels + type_count : 2 * channels + type_count + basis_count]
    columns = gain_columns(type_gain)
    for place in range(2):
        cell = jnp.where(order[1] == 0, place, 1 - place)
        acc = feat_acc[place]
        gain = dot(columns, onehot_rows(types[0, pl.ds(cell, 1), :], type_count, slots))
        half = (acc[0:slots] * gain).astype(bf16)
        grad_feat[0, cell] = (cotangent[0, cell].astype(f32) + dot(w_value[...], half).T).astype(bf16)
        grad_pos[0, cell] = acc[slots : slots + 3]


def edges(axis):
    count = lax.axis_size(axis)
    assert count % 2 == 0 and count > 2 and count & (count - 1) == 0
    even = [(i, i ^ 1) for i in range(count)]
    odd = [(i, (i + 1) % count if i % 2 else (i - 1) % count) for i in range(count)]
    return even, odd


def across(axis, step):
    return [(i, i ^ step) for i in range(lax.axis_size(axis))]


def add(a, b):
    return a.astype(f32) + b.astype(f32)


def on_device(
    features, positions, bead_types, cell_counts, w_value, w_radial, type_gain, w_out, cotangent
):
    row_count, col_count, slots, channels = features.shape
    basis_count, type_count = w_radial.shape[0], type_gain.shape[0]
    assert row_count == 1 and col_count == 2 and slots == channels == LANES
    assert 3 * type_count <= slots and type_count % 8 == 0 and basis_count == 8
    order = jnp.stack([lax.axis_index("gx") % 2, lax.axis_index("gy") % 2]).astype(jnp.int32)
    smem = pl.BlockSpec(memory_space=pltpu.SMEM)
    vmem = pl.BlockSpec(memory_space=pltpu.VMEM)
    x_even, x_odd = edges("gx")
    y_even, y_odd = edges("gy")
    cell_rows = slots + AUX
    packed = pl.pallas_call(
        pack_kernel,
        out_shape=jax.ShapeDtypeStruct((2, cell_rows, channels), bf16),
        in_specs=[smem, smem] + [vmem] * 3,
        out_specs=vmem,
        compiler_params=pltpu.CompilerParams(vmem_limit_bytes=4 * 2**20),
        name="pack",
    )(order, cell_counts, features, positions, bead_types)
    col_b = lax.ppermute(packed[0:1], "gy", y_odd)
    col_a = lax.ppermute(packed[1:2], "gy", y_even)
    own = jnp.concatenate([col_b, packed, col_a], axis=0)
    row_b = lax.ppermute(own, "gx", x_odd)
    row_a = lax.ppermute(own, "gx", x_even)
    rows = -(-(2 * channels + type_count + basis_count) // 16) * 16
    pay_rows = rows + 4 * cell_rows
    wide = 12 * slots
    span = 9 * slots
    out_feat, pay_a, pay_b, part, own_acc = pl.pallas_call(
        functools.partial(main_kernel, basis_count),
        out_shape=(
            jax.ShapeDtypeStruct(features.shape, bf16),
            jax.ShapeDtypeStruct((pay_rows, channels), bf16),
            jax.ShapeDtypeStruct((pay_rows, channels), bf16),
            jax.ShapeDtypeStruct((rows, channels), bf16),
            jax.ShapeDtypeStruct((4, cell_rows, slots), f32),
        ),
        in_specs=[smem] + [vmem] * 8,
        out_specs=(vmem,) * 5,
        scratch_shapes=[
            pltpu.VMEM((12, 8, slots), f32),
            pltpu.VMEM((2, 3, slots, slots), f32),
            pltpu.VMEM((wide, channels), bf16),
            pltpu.VMEM((wide, channels), bf16),
            pltpu.VMEM((slots, wide), bf16),
            pltpu.VMEM((channels, wide), f32),
            pltpu.VMEM((channels, wide), f32),
            pltpu.VMEM((basis_count, slots, span), bf16),
            pltpu.VMEM((slots, span), f32),
            pltpu.VMEM((slots, span), f32),
            pltpu.VMEM((slots, span), f32),
            pltpu.VMEM((basis_count, slots, channels), f32),
            pltpu.VMEM((basis_count, slots, channels), bf16),
            pltpu.VMEM((basis_count, slots, span), f32),
            pltpu.VMEM((channels, wide), f32),
            pltpu.VMEM((2, 3, slots, slots), f32),
            pltpu.VMEM((12, 3, 8, slots), f32),
        ],
        compiler_params=pltpu.CompilerParams(vmem_limit_bytes=28 * 2**20),
        name="layer",
    )(order, own, row_a, row_b, cotangent, w_value, w_radial, type_gain, w_out)

    def cells_of(block):
        return block[rows:].reshape(4, cell_rows, slots).astype(f32)

    got_b = lax.ppermute(pay_b, "gx", x_odd)
    got_a = lax.ppermute(pay_a, "gx", x_even)
    acc = own_acc + (cells_of(got_a) + cells_of(got_b))
    if len(x_even) == 4:
        other = lax.ppermute(part, "gx", across("gx", 2))
        total = add(part, got_a[:rows]) + add(other, got_b[:rows])
    else:
        total = add(part, got_a[:rows])
        step = 2
        while step < len(x_even):
            part = total.astype(bf16)
            total = add(part, lax.ppermute(part, "gx", across("gx", step)))
            step *= 2
    part = total.astype(bf16)
    got = lax.ppermute(jnp.concatenate([part, acc[3].astype(bf16)]), "gy", y_even)
    near_b = acc[2] + got[rows:].astype(f32)
    part = add(part, got[:rows]).astype(bf16)
    if len(y_even) == 4:
        sent = jnp.concatenate([part, acc[0].astype(bf16)])
        got = lax.ppermute(sent, "gy", y_odd)
        near_a = acc[1] + got[rows:].astype(f32)
        last_own, last_got = part, got[:rows]
    else:
        near_a = acc[1] + lax.ppermute(acc[0].astype(bf16), "gy", y_odd).astype(f32)
        step = 2
        while step < len(y_even):
            last_own, last_got = part, lax.ppermute(part, "gy", across("gy", step))
            part = add(last_own, last_got).astype(bf16)
            step *= 2
    grad_feat, grad_pos, wvalue, wradial, ggain, wout = pl.pallas_call(
        functools.partial(final_kernel, rows),
        out_shape=(
            jax.ShapeDtypeStruct(features.shape, bf16),
            jax.ShapeDtypeStruct(positions.shape, f32),
            jax.ShapeDtypeStruct((channels, channels), f32),
            jax.ShapeDtypeStruct((basis_count, channels), f32),
            jax.ShapeDtypeStruct((type_count, channels), f32),
            jax.ShapeDtypeStruct((channels, channels), f32),
        ),
        in_specs=[smem] + [vmem] * 7,
        out_specs=(vmem,) * 6,
        compiler_params=pltpu.CompilerParams(vmem_limit_bytes=8 * 2**20),
        name="finish",
    )(
        order, jnp.stack([near_a, near_b]), last_own, last_got, bead_types, cotangent, w_value, type_gain,
    )
    return out_feat, grad_feat, grad_pos, wvalue, wradial, ggain, wout


def solution(mesh):
    cell = P(("frame", "gx"), "gy", None, None)
    return jax.shard_map(
        on_device,
        mesh=mesh,
        in_specs=(
            cell, cell, P(("frame", "gx"), "gy", None), P(("frame", "gx"), "gy"),
            P(), P(), P(), P(), cell,
        ),
        out_specs=(cell, cell, cell) + (P("frame", None),) * 4,
        check_vma=False,
    )
```

```python
import functools
import math

import jax
import jax.numpy as jnp
from jax import lax
from jax.experimental import pallas as pl
from jax.experimental.pallas import tpu as pltpu
from jax.sharding import PartitionSpec as P

HZ = 6
SOFTEN = 0.01
FAR = 1024.0
AUX = 16
STRIP = 32
LANES = 128
LOG2E = math.log2(math.e)


f32 = jnp.float32
bf16 = jnp.bfloat16


def split3(x):
    hi = x.astype(bf16)
    rest = x - hi.astype(f32)
    mid = rest.astype(bf16)
    low = (rest - mid.astype(f32)).astype(bf16)
    return hi, mid, low


def dot(a, b):
    return jnp.dot(a, b, preferred_element_type=f32)


def dot_t(a, b):
    return lax.dot_general(a, b, (((1,), (1,)), ((), ())), preferred_element_type=f32)


def identity(size):
    rows = lax.broadcasted_iota(jnp.int32, (size, size), 0)
    lanes = lax.broadcasted_iota(jnp.int32, (size, size), 1)
    return jnp.where(rows == lanes, 1.0, 0.0).astype(bf16)


def gain_columns(type_gain):
    parts = [part.astype(f32) for part in split3(type_gain[...])]
    count, channels = type_gain.shape
    rows = jnp.concatenate(parts + [jnp.zeros((channels - 3 * count, channels), f32)], axis=0)
    return rows.T[:, 0 : 3 * count].astype(bf16)


def onehot_rows(types_row, type_count, slots):
    rows = lax.broadcasted_iota(jnp.int32, (3 * type_count, slots), 0)
    hit = (rows == types_row) | (rows == types_row + type_count) | (rows == types_row + 2 * type_count)
    return jnp.where(hit, 1.0, 0.0).astype(bf16)


def pack_kernel(
    order, counts, feat, pos, types, cotangent, w_value, w_radial, type_gain, w_out,
    packed, types_out, cotangent_out, w_value_out, w_radial_out, type_gain_out, w_out_out,
    counts_here, pos_here, sems,
):
    slots = feat.shape[2]
    moves = [(counts, counts_here), (pos, pos_here), (types, types_out)]
    for place in range(2):
        cell = jnp.where(order[1] == 0, place, 1 - place)
        moves.append((feat.at[0, cell], packed.at[place, 0:slots, :]))
    moves += [
        (w_value, w_value_out), (type_gain, type_gain_out), (cotangent, cotangent_out),
        (w_radial, w_radial_out), (w_out, w_out_out),
    ]
    copies = [pltpu.make_async_copy(a, b, sems.at[i]) for i, (a, b) in enumerate(moves)]
    for copy in copies:
        copy.start()
    for copy in copies[:3]:
        copy.wait()
    for place in range(2):
        cell = jnp.where(order[1] == 0, place, 1 - place)
        lane = lax.broadcasted_iota(jnp.int32, (1, slots), 1)
        valid = lane < counts_here[0, cell]
        parts = [[], [], []]
        for comp in range(3):
            row = pos_here[0, comp, pl.ds(cell, 1), :]
            if comp == 2:
                row = row * float(HZ)
            row = jnp.where(valid, row, -FAR)
            for which, part in enumerate(split3(row)):
                parts[which].append(part.astype(f32))
        rows = parts[0] + parts[1] + parts[2]
        rows.append(types_out[0, pl.ds(cell, 1), :].astype(f32))
        rows.append(jnp.zeros((AUX - len(rows), slots), f32))
        packed[place, slots : slots + AUX, :] = jnp.concatenate(rows, axis=0).astype(bf16)
    for copy in copies[3:]:
        copy.wait()


def pair_terms(near_pos, index, own_xyz, is_self, first_row, basis_count):
    n1 = float(basis_count - 1)
    gamma = 0.5 * n1 * n1
    delta = [near_pos[index, comp : comp + 1, :] - own_xyz[comp] for comp in range(3)]
    dist_sq = delta[0] * delta[0] + delta[1] * delta[1] + delta[2] * delta[2]
    dist_sq = jnp.minimum(dist_sq, 1.0)
    inside = 1.0 - dist_sq
    radius_sq = dist_sq + SOFTEN
    inverse = lax.rsqrt(radius_sq)
    radius = radius_sq * inverse
    gauss = jnp.exp2(radius_sq * (-gamma * LOG2E))
    step = jnp.exp2(radius * (n1 * LOG2E))
    if is_self:
        rows = first_row + lax.broadcasted_iota(jnp.int32, gauss.shape, 0)
        lanes = lax.broadcasted_iota(jnp.int32, gauss.shape, 1)
        gauss = jnp.where(rows == lanes, 0.0, gauss)
    part = inside * gauss
    weight = inside * part
    value_factor = part * (inside * -n1 - 2.0 * n1 / gamma)
    slope_factor = weight * (inverse * step)
    return step, weight, value_factor, slope_factor


def near_cell(aux, row, col, order):
    sx = jnp.where(order[0] == 0, 1.0, -1.0).astype(f32)
    sy = jnp.where(order[1] == 0, 1.0, -1.0).astype(f32)
    aux = aux.astype(f32)
    xyz = aux[0:3] + aux[3:6] + aux[6:9]
    x = xyz[0:1] + sx * float(1 - row)
    y = xyz[1:2] + sy * float(col)
    return [x, y, xyz[2:3]], xyz[0:1] < -0.5 * FAR, aux[9:10].astype(jnp.int32)


def strip_of(s):
    first = pl.multiple_of(s * STRIP, STRIP)
    return first, pl.ds(first, STRIP)


def stage(count, *steps):
    def body(s, carry):
        for step in steps:
            step(s)
        return carry

    lax.fori_loop(0, count, body, 0)


def fill_pairs(basis_count, slots, near_pos, own_pos, place, self_block, terms, weights, s):
    first, strip = strip_of(s)
    own_xyz = [own_pos[place, comp, strip, :] for comp in range(3)]
    for block in range(weights.shape[1] // slots):
        there = slice(block * slots, (block + 1) * slots)
        step, weight, value_factor, slope_factor = pair_terms(
            near_pos, block, own_xyz, block == self_block, first, basis_count
        )
        terms[0, strip, there] = step
        terms[1, strip, there] = value_factor
        terms[2, strip, there] = slope_factor
        for k in range(basis_count):
            rows = pl.ds(pl.multiple_of(first + k * slots, STRIP), STRIP)
            weights[rows, there] = weight.astype(bf16)
            if k < basis_count - 1:
                weight = weight * step


def carry_values(slots, value_t, gain_t, eye, near, here):
    near_feat, near_val, carried_t, onehot, projected, gains = near
    proj = dot_t(value_t, near_feat[here, :])
    gain = dot(gain_t, onehot[:, here])
    projected[:, here] = proj
    gains[:, here] = gain
    carried = (proj * gain).astype(bf16)
    carried_t[:, here] = carried
    for first in range(here.start, here.stop, slots):
        there = slice(first - here.start, first - here.start + slots)
        near_val[first : first + slots, :] = dot_t(eye, carried[:, there]).astype(bf16)


def chunk_of(s, size):
    return pl.ds(pl.multiple_of(s * size, size), size)


def early_kernel(
    basis_count, order, own, row_a, row_b, w_value, type_gain,
    near_pos, own_pos, near_feat, near_val, carried_t, onehot, projected, gains,
    weights_b, weights_a, terms_b, terms_a, summed_b, summed_a,
):
    slots = near_feat.shape[1]
    strips = slots // STRIP
    chunk = basis_count * slots // strips
    weights, terms, summed = (weights_b, weights_a), (terms_b, terms_a), (summed_b, summed_a)
    for index in range(6):
        col, row = index // 3 + 1, index % 3
        ref = (row_a, own, row_b)[row]
        here = slice(index * slots, (index + 1) * slots)
        near_feat[here, :] = ref[col - 1, 0:slots, :]
        xyz, unused, types = near_cell(ref[col - 1, slots : slots + AUX, :], row, col, order)
        onehot[:, here] = onehot_rows(types, type_gain.shape[0], slots)
        for comp in range(3):
            near_pos[index, comp : comp + 1, :] = xyz[comp]
            if row == 1:
                line = jnp.where(unused, FAR, xyz[comp])
                own_pos[col - 1, comp] = jnp.broadcast_to(line, (slots, slots)).T
    near = (near_feat, near_val, carried_t, onehot, projected, gains)
    value_t = w_value[...].astype(f32).T.astype(bf16)
    carry_values(slots, value_t, gain_columns(type_gain), identity(slots), near, slice(0, 6 * slots))

    def sums(place, s):
        rows = chunk_of(s, chunk)
        summed[place][:, rows] = dot_t(carried_t[...], weights[place][rows, :])

    def pairs(place, s):
        fill_pairs(
            basis_count, slots, near_pos, own_pos, place, 3 * place + 1, terms[place], weights[place], s
        )

    run = functools.partial
    stage(strips, run(pairs, 0))
    stage(strips, run(sums, 0), run(pairs, 1))
    stage(strips, run(sums, 1))


def main_kernel(
    basis_count, order, col_a, col_b, cotangent, w_value, w_radial, type_gain, w_out,
    in_pos, own_pos, in_feat, in_val, in_carried_t, in_onehot, in_projected, in_gains,
    in_weights_b, in_weights_a, in_terms_b, in_terms_a, in_summed_b, in_summed_a,
    out_feat, keep, pay_a, pay_b, fold_a, fold_b, own_acc,
    out_pos, ot_feat, ot_val, ot_carried_t, ot_onehot, ot_projected, ot_gains, columns, products, whole,
    ot_weights_b, ot_weights_a, ot_terms_b, ot_terms_a, summed_b, summed_a,
    scaled_b, scaled_a, scaled_tb, scaled_ta,
    in_grad_b, in_grad_a, ot_grad_b, ot_grad_a, in_back, ot_back, pull_own, pull_far,
):
    slots, channels = cotangent.shape[2], cotangent.shape[3]
    type_count = type_gain.shape[0]
    third = 3 * slots
    strips = slots // STRIP
    chunk = basis_count * slots // strips
    in_weights, ot_weights = (in_weights_b, in_weights_a), (ot_weights_b, ot_weights_a)
    in_terms, ot_terms = (in_terms_b, in_terms_a), (ot_terms_b, ot_terms_a)
    in_summed, summed = (in_summed_b, in_summed_a), (summed_b, summed_a)
    scaled, scaled_t = (scaled_b, scaled_a), (scaled_tb, scaled_ta)
    in_grad, ot_grad = (in_grad_b, in_grad_a), (ot_grad_b, ot_grad_a)
    for index in range(6):
        place, row = index // 3, index % 3
        ref = (col_b, col_a)[place]
        here = slice(index * slots, (index + 1) * slots)
        ot_feat[here, :] = ref[row, 0:slots, :]
        xyz, _, types = near_cell(ref[row, slots : slots + AUX, :], row, 3 * place, order)
        ot_onehot[:, here] = onehot_rows(types, type_count, slots)
        for comp in range(3):
            out_pos[index, comp : comp + 1, :] = xyz[comp]
    scale = [math.exp(-0.5 * k * k) for k in range(basis_count)]
    radial = [w_radial[k : k + 1, :] * scale[k] for k in range(basis_count)]
    radial_t = jnp.concatenate(radial + [jnp.zeros((channels - basis_count, channels), f32)], axis=0).T
    for k in range(basis_count):
        columns[k] = jnp.broadcast_to(radial_t[:, k : k + 1], (channels, slots))
    near = (ot_feat, ot_val, ot_carried_t, ot_onehot, ot_projected, ot_gains)
    value_t = w_value[...].astype(f32).T.astype(bf16)
    carry_values(slots, value_t, gain_columns(type_gain), identity(slots), near, slice(0, 6 * slots))

    def outer(place):
        return slice(place * third, (place + 1) * third)

    def pairs(place, s):
        cells = out_pos.at[place * 3 : place * 3 + 3]
        fill_pairs(basis_count, slots, cells, own_pos, place, -1, ot_terms[place], ot_weights[place], s)

    def sums(place, s):
        rows = chunk_of(s, chunk)
        summed[place][:, rows] = in_summed[place][:, rows] + dot_t(
            ot_carried_t[:, outer(place)], ot_weights[place][rows, :]
        )

    def epilogue(place):
        aggregate_t = None
        for k in range(basis_count):
            term = summed[place][:, k * slots : (k + 1) * slots] * columns[k]
            aggregate_t = term if aggregate_t is None else aggregate_t + term
        agg_half = aggregate_t.T.astype(bf16)
        cell = jnp.where(order[1] == 0, place, 1 - place)
        pre_act = dot(agg_half, w_out[...])
        sig = jax.nn.sigmoid(pre_act)
        center = in_feat[(3 * place + 1) * slots : (3 * place + 2) * slots, :]
        out_feat[0, cell] = (center.astype(f32) + pre_act * sig).astype(bf16)
        grad_pre = (
            cotangent[0, cell].astype(f32) * sig * (1.0 + pre_act * (1.0 - sig))
        ).astype(bf16)
        agg = dot_t(grad_pre, w_out[...]).astype(bf16).astype(f32)
        agg_t = agg.T
        for k in range(basis_count):
            here = slice(k * slots, (k + 1) * slots)
            scaled[place][here, :] = (agg * radial[k]).astype(bf16)
            scaled_t[place][:, here] = (agg_t * columns[k]).astype(bf16)
            product = agg_t * summed[place][:, here]
            products[:, here] = product if place == 0 else products[:, here] + product
        return dot(aggregate_t.astype(bf16), grad_pre)

    def weight_grads(place, s):
        rows = chunk_of(s, chunk)
        in_grad[place][rows, :] = dot_t(scaled[place][rows, :], in_val[...])
        ot_grad[place][rows, :] = dot_t(scaled[place][rows, :], ot_val[outer(place), :])

    def pulls(place, s):
        first, strip = strip_of(s)
        own_xyz = [own_pos[place, comp, strip, :] for comp in range(3)]
        total = [jnp.zeros((STRIP, slots), f32) for _ in range(3)]
        for block in range(9):
            inner = block < 6
            grad = (in_grad if inner else ot_grad)[place]
            terms = (in_terms if inner else ot_terms)[place]
            cells = in_pos if inner else out_pos
            cell = block if inner else place * 3 + block - 6
            index = block if inner else 6 + cell
            local = block if inner else block - 6
            there = slice(local * slots, (local + 1) * slots)

            def grad_of(k):
                rows = pl.ds(pl.multiple_of(first + k * slots, STRIP), STRIP)
                return grad[rows, there]

            step = terms[0, strip, there]
            value = grad_of(basis_count - 1)
            slope = None
            for k in range(basis_count - 2, -1, -1):
                slope = value if slope is None else value + step * slope
                value = grad_of(k) + step * value
            pull = terms[1, strip, there] * value + terms[2, strip, there] * slope
            for comp in range(3):
                force = pull * (cells[cell, comp : comp + 1, :] - own_xyz[comp])
                total[comp] = total[comp] + force
                pull_far[index, comp] += (force[0:8] + force[8:16]) + (force[16:24] + force[24:32])
        for comp in range(3):
            pull_own[place, comp, strip, :] = total[comp]

    def value_grads(s):
        rows = chunk_of(s, chunk)
        parts = [scaled_t[place][:, rows] for place in range(2)]
        in_back[...] += dot(parts[0], in_weights[0][rows, :]) + dot(parts[1], in_weights[1][rows, :])
        for place in range(2):
            ot_back[:, outer(place)] += dot(parts[place], ot_weights[place][rows, :])

    run = functools.partial
    pull_far[...] = jnp.zeros_like(pull_far)
    in_back[...] = jnp.zeros_like(in_back)
    ot_back[...] = jnp.zeros_like(ot_back)
    stage(strips, run(pairs, 0))
    stage(strips, run(sums, 0), run(pairs, 1))
    for s in range(strips):
        sums(1, s)
    wout = epilogue(0)
    for s in range(strips):
        weight_grads(0, s)
    wout = wout + epilogue(1)
    stage(strips, run(weight_grads, 1), run(pulls, 0))
    stage(strips, value_grads, run(pulls, 1))

    wvalue = ggain = None
    for back, feat, onehot, projected, gains in (
        (in_back, in_feat, in_onehot, in_projected, in_gains),
        (ot_back, ot_feat, ot_onehot, ot_projected, ot_gains),
    ):
        half = (back[...] * gains[...]).astype(bf16)
        hi, mid, _ = split3(back[...] * projected[...])
        wvalue_part = dot(half, feat[...])
        ggain_part = dot_t(hi, onehot[...]) + dot_t(mid, onehot[...])
        wvalue = wvalue_part if wvalue is None else wvalue + wvalue_part
        ggain = ggain_part if ggain is None else ggain + ggain_part
    ggain = jnp.concatenate([ggain, jnp.zeros((channels, slots - ggain.shape[1]), f32)], axis=1).T
    group = lax.broadcasted_iota(jnp.int32, (basis_count, basis_count * slots), 1) // slots
    mine = lax.broadcasted_iota(jnp.int32, (basis_count, basis_count * slots), 0)
    select = jnp.where(group == mine, 1.0, 0.0).astype(bf16)
    hi, mid, _ = split3(products[...])
    wradial = dot_t(select, hi) + dot_t(select, mid)
    wradial = jnp.concatenate([wradial[k : k + 1] * scale[k] for k in range(basis_count)], axis=0)
    pad = 2 * keep.shape[0] - 2 * channels - type_count - basis_count
    tail = [ggain[0:type_count], wradial] + ([jnp.zeros((pad, channels), f32)] if pad else [])
    full = jnp.concatenate([wvalue.T, wout] + tail, axis=0).astype(bf16)
    rows = keep.shape[0]
    whole[0] = full[0:rows]
    whole[1] = full[rows : 2 * rows]
    keep[...] = whole[order[0]]
    for ref in (pay_a, pay_b):
        ref[0:rows, :] = whole[1 - order[0]]
    force = float(basis_count - 1)
    size = slots + AUX
    for col in range(4):
        for row in range(3):
            inner = col in (1, 2)
            local = (col - 1) * 3 + row if inner else (0 if col == 0 else 3) + row
            back = (in_back if inner else ot_back)[:, local * slots : (local + 1) * slots]
            lines = []
            for comp in range(3):
                line = jnp.sum(pull_far[local if inner else 6 + local, comp], axis=0, keepdims=True)
                if row == 1 and inner:
                    line = line - jnp.sum(pull_own[col - 1, comp].T, axis=0, keepdims=True)
                lines.append(line * (force * HZ if comp == 2 else force))
            lines.append(jnp.zeros((AUX - 3, slots), f32))
            lines = jnp.concatenate(lines, axis=0)
            if row == 1:
                own_acc[col, 0:slots, :] = back
                own_acc[col, slots:size, :] = lines
                continue
            if inner:
                ref, base = (fold_a if row == 0 else fold_b), (col - 1) * size
            else:
                ref, base = (pay_a if row == 0 else pay_b), rows + (0 if col == 0 else size)
            ref[base : base + slots, :] = back.astype(bf16)
            ref[base + slots : base + size, :] = lines.astype(bf16)


def cell_grads(own, got_a, got_b, got, types_row, cotangent, w_value, type_gain):
    slots = cotangent.shape[0]
    total = own + (got_a.astype(f32) + got_b.astype(f32)) + got.astype(f32)
    gain = dot(gain_columns(type_gain), onehot_rows(types_row, type_gain.shape[0], slots))
    half = (total[0:slots] * gain).astype(bf16)
    feat = (cotangent.astype(f32) + dot(w_value[...], half).T).astype(bf16)
    return feat, total[slots : slots + 3]


def near_side_kernel(order, own, got_a, got_b, got, types, cotangent, w_value, type_gain, feat, pos):
    cell = 1 - order[1]
    feat[...], pos[0:3, :] = cell_grads(
        own[...], got_a[...], got_b[...], got[...], types[0, pl.ds(cell, 1), :], cotangent[0, cell],
        w_value, type_gain,
    )


def far_side_kernel(
    order, own, got_a, got_b, got, types, cotangent, w_value, type_gain, other_feat, other_pos,
    grad_feat, grad_pos,
):
    cell = order[1]
    feat, pos = cell_grads(
        own[...], got_a[...], got_b[...], got[...], types[0, pl.ds(cell, 1), :], cotangent[0, cell],
        w_value, type_gain,
    )
    grad_feat[0, cell] = feat
    grad_feat[0, 1 - cell] = other_feat[...]
    for comp in range(3):
        grad_pos[0, comp, pl.ds(cell, 1), :] = pos[comp : comp + 1]
        grad_pos[0, comp, pl.ds(1 - cell, 1), :] = other_pos[comp : comp + 1, :]


def weights_kernel(order, mine, other, wvalue, wradial, ggain, wout):
    first = order[0] == 0
    low = jnp.where(first, mine[...], other[...])
    high = jnp.where(first, other[...], mine[...])
    total = jnp.concatenate([low, high], axis=0)
    base = 0
    for ref in (wvalue, wout, ggain, wradial):
        ref[...] = total[base : base + ref.shape[0]]
        base += ref.shape[0]


def edges(axis):
    count = lax.axis_size(axis)
    assert count % 2 == 0 and count > 2 and count & (count - 1) == 0
    even = [(i, i ^ 1) for i in range(count)]
    odd = [(i, (i + 1) % count if i % 2 else (i - 1) % count) for i in range(count)]
    return even, odd


def across(axis, step):
    return [(i, i ^ step) for i in range(lax.axis_size(axis))]


def add(a, b):
    return a.astype(f32) + b.astype(f32)


def on_device(
    features, positions, bead_types, cell_counts, w_value, w_radial, type_gain, w_out, cotangent
):
    row_count, col_count, slots, channels = features.shape
    basis_count, type_count = w_radial.shape[0], type_gain.shape[0]
    assert row_count == 1 and col_count == 2 and slots == channels == LANES
    assert 3 * type_count <= slots and type_count % 8 == 0 and basis_count == 8
    order = jnp.stack([lax.axis_index("gx") % 2, lax.axis_index("gy") % 2]).astype(jnp.int32)
    smem = pl.BlockSpec(memory_space=pltpu.SMEM)
    vmem = pl.BlockSpec(memory_space=pltpu.VMEM)
    x_even, x_odd = edges("gx")
    y_even, y_odd = edges("gy")
    size = slots + AUX
    inner, outer, tall = 6 * slots, 3 * slots, basis_count * slots
    rows = -(-(2 * channels + type_count + basis_count) // 32) * 16
    kinds = 3 * type_count
    shape = jax.ShapeDtypeStruct

    def call(kernel, name, mib, out_shape, arrays, scratch=()):
        return pl.pallas_call(
            kernel,
            out_shape=out_shape,
            in_specs=[smem] + [vmem] * len(arrays),
            out_specs=jax.tree.map(lambda _: vmem, out_shape),
            scratch_shapes=list(scratch),
            compiler_params=pltpu.CompilerParams(vmem_limit_bytes=mib * 2**20),
            name=name,
        )(order, *arrays)

    hbm = pl.BlockSpec(memory_space=pltpu.HBM)
    packed, bead_types, cotangent, w_value, w_radial, type_gain, w_out = pl.pallas_call(
        pack_kernel,
        out_shape=(
            shape((2, size, channels), bf16),
            *(shape(a.shape, a.dtype) for a in (bead_types, cotangent, w_value, w_radial, type_gain, w_out)),
        ),
        in_specs=[smem] + [hbm] * 9,
        out_specs=(vmem,) * 7,
        scratch_shapes=[
            pltpu.SMEM(cell_counts.shape, jnp.int32),
            pltpu.VMEM((row_count, 3, col_count, slots), f32),
            pltpu.SemaphoreType.DMA((10,)),
        ],
        compiler_params=pltpu.CompilerParams(vmem_limit_bytes=4 * 2**20),
        name="pack",
    )(
        order,
        *(
            pltpu.with_memory_space_constraint(a, pltpu.HBM)
            for a in (
                cell_counts, features, jnp.swapaxes(positions, 1, 2), bead_types, cotangent, w_value,
                w_radial, type_gain, w_out,
            )
        ),
    )
    row_b = lax.ppermute(packed, "gx", x_odd)
    row_a = lax.ppermute(packed, "gx", x_even)
    col_b = lax.ppermute(jnp.stack([row_a[0], packed[0], row_b[0]]), "gy", y_odd)
    col_a = lax.ppermute(jnp.stack([row_a[1], packed[1], row_b[1]]), "gy", y_even)
    early = call(
        functools.partial(early_kernel, basis_count), "early", 8,
        (
            shape((6, 8, slots), f32),
            shape((2, 3, slots, slots), f32),
            shape((inner, channels), bf16),
            shape((inner, channels), bf16),
            shape((channels, inner), bf16),
            shape((kinds, inner), bf16),
            shape((channels, inner), f32),
            shape((channels, inner), f32),
        )
        + (shape((tall, inner), bf16),) * 2
        + (shape((3, slots, inner), f32),) * 2
        + (shape((channels, tall), f32),) * 2,
        (packed, row_a, row_b, w_value, type_gain),
    )
    out_feat, keep, pay_a, pay_b, fold_a, fold_b, own_acc = call(
        functools.partial(main_kernel, basis_count), "layer", 28,
        (
            shape(features.shape, bf16),
            shape((rows, channels), bf16),
            shape((rows + 2 * size, channels), bf16),
            shape((rows + 2 * size, channels), bf16),
            shape((2 * size, channels), bf16),
            shape((2 * size, channels), bf16),
            shape((4, size, slots), f32),
        ),
        (col_a, col_b, cotangent, w_value, w_radial, type_gain, w_out) + tuple(early),
        [
            pltpu.VMEM((6, 8, slots), f32),
            pltpu.VMEM((2 * outer, channels), bf16),
            pltpu.VMEM((2 * outer, channels), bf16),
            pltpu.VMEM((channels, 2 * outer), bf16),
            pltpu.VMEM((kinds, 2 * outer), bf16),
            pltpu.VMEM((channels, 2 * outer), f32),
            pltpu.VMEM((channels, 2 * outer), f32),
            pltpu.VMEM((basis_count, channels, slots), f32),
            pltpu.VMEM((channels, tall), f32),
            pltpu.VMEM((2, rows, channels), bf16),
        ]
        + [pltpu.VMEM((tall, outer), bf16)] * 2
        + [pltpu.VMEM((3, slots, outer), f32)] * 2
        + [pltpu.VMEM((channels, tall), f32)] * 2
        + [pltpu.VMEM((tall, channels), bf16)] * 2
        + [pltpu.VMEM((channels, tall), bf16)] * 2
        + [pltpu.VMEM((tall, inner), f32)] * 2
        + [pltpu.VMEM((tall, outer), f32)] * 2
        + [
            pltpu.VMEM((channels, inner), f32),
            pltpu.VMEM((channels, 2 * outer), f32),
            pltpu.VMEM((2, 3, slots, slots), f32),
            pltpu.VMEM((12, 3, 8, slots), f32),
        ],
    )
    got_b = lax.ppermute(pay_b, "gx", x_odd)
    got_a = lax.ppermute(pay_a, "gx", x_even)
    if len(x_even) == 4:
        other = lax.ppermute(keep, "gx", across("gx", 2))
        total = add(keep, got_a[:rows]) + add(other, got_b[:rows])
    else:
        total = add(keep, got_a[:rows])
        step = 2
        while step < len(x_even):
            part = total.astype(bf16)
            total = add(part, lax.ppermute(part, "gx", across("gx", step)))
            step *= 2
    part = total.astype(bf16)
    corner_b = own_acc[0] + add(got_a[rows : rows + size], got_b[rows : rows + size])
    corner_a = own_acc[3] + add(got_a[rows + size :], got_b[rows + size :])
    got = lax.ppermute(jnp.concatenate([part, corner_a.astype(bf16)]), "gy", y_even)
    fold_a, fold_b, got_a, got_b = lax.optimization_barrier((fold_a, fold_b, got_a, got_b))
    own_b = lax.ppermute(fold_b, "gx", x_odd)
    own_a = lax.ppermute(fold_a, "gx", x_even)
    cell_args = (bead_types, cotangent, w_value, type_gain)
    near_feat, near_pos = call(
        near_side_kernel, "near_side", 4,
        (shape((slots, channels), bf16), shape((8, slots), f32)),
        (own_acc[2], own_a[size:], own_b[size:], got[rows:]) + cell_args,
    )
    part = add(part, got[:rows]).astype(bf16)
    if len(y_even) == 4:
        got = lax.ppermute(jnp.concatenate([part, corner_b.astype(bf16)]), "gy", y_odd)
        total, far = add(part, got[:rows]), got[rows:]
    else:
        far = lax.ppermute(corner_b.astype(bf16), "gy", y_odd)
        step = 2
        while step < len(y_even):
            total = add(part, lax.ppermute(part, "gy", across("gy", step)))
            part = total.astype(bf16)
            step *= 2
    half = lax.ppermute(total, "gx", x_even)
    grad_feat, grad_pos = call(
        far_side_kernel, "far_side", 4,
        (shape(features.shape, bf16), shape((row_count, 3, col_count, slots), f32)),
        (own_acc[1], own_a[:size], own_b[:size], far) + cell_args + (near_feat, near_pos),
    )
    wvalue, wradial, ggain, wout = call(
        weights_kernel, "weights", 4,
        (
            shape((channels, channels), f32),
            shape((basis_count, channels), f32),
            shape((type_count, channels), f32),
            shape((channels, channels), f32),
        ),
        (total, half),
    )
    return out_feat, grad_feat, jnp.swapaxes(grad_pos, 1, 2), wvalue, wradial, ggain, wout


def solution(mesh):
    cell = P(("frame", "gx"), "gy", None, None)
    return jax.shard_map(
        on_device,
        mesh=mesh,
        in_specs=(
            cell, cell, P(("frame", "gx"), "gy", None), P(("frame", "gx"), "gy"),
            P(), P(), P(), P(), cell,
        ),
        out_specs=(cell, cell, cell) + (P("frame", None),) * 4,
        check_vma=False,
    )
```

```python
import functools
import math

import jax
import jax.numpy as jnp
from jax import lax
from jax.experimental import pallas as pl
from jax.experimental.pallas import tpu as pltpu
from jax.sharding import PartitionSpec as P


HZ = 6
SOFTEN = 0.01
FAR = 1024.0
AUX = 16
STRIP = 32
LANES = 128
LOG2E = math.log2(math.e)


f32 = jnp.float32
bf16 = jnp.bfloat16


def split3(x):
    hi = x.astype(bf16)
    rest = x - hi.astype(f32)
    mid = rest.astype(bf16)
    low = (rest - mid.astype(f32)).astype(bf16)
    return hi, mid, low


def dot(a, b):
    return jnp.dot(a, b, preferred_element_type=f32)


def dot_t(a, b):
    return lax.dot_general(a, b, (((1,), (1,)), ((), ())), preferred_element_type=f32)


def identity(size):
    rows = lax.broadcasted_iota(jnp.int32, (size, size), 0)
    lanes = lax.broadcasted_iota(jnp.int32, (size, size), 1)
    return jnp.where(rows == lanes, 1.0, 0.0).astype(bf16)


def gain_columns(type_gain):
    parts = [part.astype(f32) for part in split3(type_gain[...])]
    count, channels = type_gain.shape
    rows = jnp.concatenate(parts + [jnp.zeros((channels - 3 * count, channels), f32)], axis=0)
    return rows.T[:, 0 : 3 * count].astype(bf16)


def onehot_rows(types_row, type_count, slots):
    rows = lax.broadcasted_iota(jnp.int32, (3 * type_count, slots), 0)
    hit = (rows == types_row) | (rows == types_row + type_count) | (rows == types_row + 2 * type_count)
    return jnp.where(hit, 1.0, 0.0).astype(bf16)


def pack_kernel(
    order, counts, feat, pos, types, cotangent, w_value, w_radial, type_gain, w_out,
    packed, types_out, cotangent_out, w_value_out, w_radial_out, type_gain_out, w_out_out,
    counts_here, pos_here, sems,
):
    slots = feat.shape[2]
    moves = [(counts, counts_here), (pos, pos_here), (types, types_out)]
    for place in range(2):
        cell = jnp.where(order[1] == 0, place, 1 - place)
        moves.append((feat.at[0, cell], packed.at[place, 0:slots, :]))
    moves += [
        (w_value, w_value_out), (type_gain, type_gain_out), (cotangent, cotangent_out),
        (w_radial, w_radial_out), (w_out, w_out_out),
    ]
    copies = [pltpu.make_async_copy(a, b, sems.at[i]) for i, (a, b) in enumerate(moves)]
    for copy in copies:
        copy.start()
    for copy in copies[:3]:
        copy.wait()
    for place in range(2):
        cell = jnp.where(order[1] == 0, place, 1 - place)
        lane = lax.broadcasted_iota(jnp.int32, (1, slots), 1)
        valid = lane < counts_here[0, cell]
        parts = [[], [], []]
        for comp in range(3):
            row = pos_here[0, comp, pl.ds(cell, 1), :]
            if comp == 2:
                row = row * float(HZ)
            row = jnp.where(valid, row, -FAR)
            for which, part in enumerate(split3(row)):
                parts[which].append(part.astype(f32))
        rows = parts[0] + parts[1] + parts[2]
        rows.append(types_out[0, pl.ds(cell, 1), :].astype(f32))
        rows.append(jnp.zeros((AUX - len(rows), slots), f32))
        packed[place, slots : slots + AUX, :] = jnp.concatenate(rows, axis=0).astype(bf16)
    for copy in copies[3:]:
        copy.wait()


def pair_terms(near_pos, index, own_xyz, is_self, first_row, basis_count):
    n1 = float(basis_count - 1)
    gamma = 0.5 * n1 * n1
    delta = [near_pos[index, comp : comp + 1, :] - own_xyz[comp] for comp in range(3)]
    dist_sq = delta[0] * delta[0] + delta[1] * delta[1] + delta[2] * delta[2]
    dist_sq = jnp.minimum(dist_sq, 1.0)
    inside = 1.0 - dist_sq
    radius_sq = dist_sq + SOFTEN
    inverse = lax.rsqrt(radius_sq)
    radius = radius_sq * inverse
    gauss = jnp.exp2(radius_sq * (-gamma * LOG2E))
    step = jnp.exp2(radius * (n1 * LOG2E))
    if is_self:
        rows = first_row + lax.broadcasted_iota(jnp.int32, gauss.shape, 0)
        lanes = lax.broadcasted_iota(jnp.int32, gauss.shape, 1)
        gauss = jnp.where(rows == lanes, 0.0, gauss)
    part = inside * gauss
    weight = inside * part
    value_factor = part * (inside * -n1 - 2.0 * n1 / gamma)
    slope_factor = weight * (inverse * step)
    return step, weight, value_factor, slope_factor


def near_cell(aux, row, col, order):
    sx = jnp.where(order[0] == 0, 1.0, -1.0).astype(f32)
    sy = jnp.where(order[1] == 0, 1.0, -1.0).astype(f32)
    aux = aux.astype(f32)
    xyz = aux[0:3] + aux[3:6] + aux[6:9]
    x = xyz[0:1] + sx * float(1 - row)
    y = xyz[1:2] + sy * float(col)
    return [x, y, xyz[2:3]], xyz[0:1] < -0.5 * FAR, aux[9:10].astype(jnp.int32)


def strip_of(s):
    first = pl.multiple_of(s * STRIP, STRIP)
    return first, pl.ds(first, STRIP)


def stage(count, *steps):
    def body(s, carry):
        for step in steps:
            step(s)
        return carry

    lax.fori_loop(0, count, body, 0)


def fill_pairs(basis_count, slots, near_pos, own_pos, place, self_block, terms, weights, s):
    first, strip = strip_of(s)
    own_xyz = [own_pos[place, comp, strip, :] for comp in range(3)]
    for block in range(weights.shape[1] // slots):
        there = slice(block * slots, (block + 1) * slots)
        step, weight, value_factor, slope_factor = pair_terms(
            near_pos, block, own_xyz, block == self_block, first, basis_count
        )
        terms[0, strip, there] = step
        terms[1, strip, there] = value_factor
        terms[2, strip, there] = slope_factor
        for k in range(basis_count):
            rows = pl.ds(pl.multiple_of(first + k * slots, STRIP), STRIP)
            weights[rows, there] = weight.astype(bf16)
            if k < basis_count - 1:
                weight = weight * step


def carry_values(slots, value_t, gain_t, eye, near, here):
    near_feat, near_val, carried_t, onehot, projected, gains = near
    proj = dot_t(value_t, near_feat[here, :])
    gain = dot(gain_t, onehot[:, here])
    projected[:, here] = proj
    gains[:, here] = gain
    carried = (proj * gain).astype(bf16)
    carried_t[:, here] = carried
    for first in range(here.start, here.stop, slots):
        there = slice(first - here.start, first - here.start + slots)
        near_val[first : first + slots, :] = dot_t(eye, carried[:, there]).astype(bf16)


def chunk_of(s, size):
    return pl.ds(pl.multiple_of(s * size, size), size)


def early_kernel(
    basis_count, order, own, row_a, row_b, w_value, type_gain,
    near_pos, own_pos, near_feat, near_val, carried_t, onehot, projected, gains,
    weights_b, weights_a, terms_b, terms_a, summed_b, summed_a,
):
    slots = near_feat.shape[1]
    strips = slots // STRIP
    chunk = basis_count * slots // strips
    weights, terms, summed = (weights_b, weights_a), (terms_b, terms_a), (summed_b, summed_a)
    for index in range(6):
        col, row = index // 3 + 1, index % 3
        ref = (row_a, own, row_b)[row]
        here = slice(index * slots, (index + 1) * slots)
        near_feat[here, :] = ref[col - 1, 0:slots, :]
        xyz, unused, types = near_cell(ref[col - 1, slots : slots + AUX, :], row, col, order)
        onehot[:, here] = onehot_rows(types, type_gain.shape[0], slots)
        for comp in range(3):
            near_pos[index, comp : comp + 1, :] = xyz[comp]
            if row == 1:
                line = jnp.where(unused, FAR, xyz[comp])
                own_pos[col - 1, comp] = jnp.broadcast_to(line, (slots, slots)).T
    near = (near_feat, near_val, carried_t, onehot, projected, gains)
    value_t = w_value[...].astype(f32).T.astype(bf16)
    carry_values(slots, value_t, gain_columns(type_gain), identity(slots), near, slice(0, 6 * slots))

    def sums(place, s):
        rows = chunk_of(s, chunk)
        summed[place][:, rows] = dot_t(carried_t[...], weights[place][rows, :])

    def pairs(place, s):
        fill_pairs(
            basis_count, slots, near_pos, own_pos, place, 3 * place + 1, terms[place], weights[place], s
        )

    run = functools.partial
    stage(strips, run(pairs, 0))
    stage(strips, run(sums, 0), run(pairs, 1))
    stage(strips, run(sums, 1))


def main_kernel(
    basis_count, order, col_a, col_b, cotangent, w_value, w_radial, type_gain, w_out,
    in_pos, own_pos, in_feat, in_val, in_carried_t, in_onehot, in_projected, in_gains,
    in_weights_b, in_weights_a, in_terms_b, in_terms_a, in_summed_b, in_summed_a,
    out_feat, keep, pay_a, pay_b, fold_a, fold_b, own_acc,
    out_pos, ot_feat, ot_val, ot_carried_t, ot_onehot, ot_projected, ot_gains, columns, products, whole,
    ot_weights_b, ot_weights_a, ot_terms_b, ot_terms_a, summed_b, summed_a,
    scaled_b, scaled_a, scaled_tb, scaled_ta,
    in_grad_b, in_grad_a, ot_grad_b, ot_grad_a, in_back, ot_back, pull_own, pull_far,
):
    slots, channels = cotangent.shape[2], cotangent.shape[3]
    type_count = type_gain.shape[0]
    third = 3 * slots
    strips = slots // STRIP
    chunk = basis_count * slots // strips
    in_weights, ot_weights = (in_weights_b, in_weights_a), (ot_weights_b, ot_weights_a)
    in_terms, ot_terms = (in_terms_b, in_terms_a), (ot_terms_b, ot_terms_a)
    in_summed, summed = (in_summed_b, in_summed_a), (summed_b, summed_a)
    scaled, scaled_t = (scaled_b, scaled_a), (scaled_tb, scaled_ta)
    in_grad, ot_grad = (in_grad_b, in_grad_a), (ot_grad_b, ot_grad_a)
    for index in range(6):
        place, row = index // 3, index % 3
        ref = (col_b, col_a)[place]
        here = slice(index * slots, (index + 1) * slots)
        ot_feat[here, :] = ref[row, 0:slots, :]
        xyz, _, types = near_cell(ref[row, slots : slots + AUX, :], row, 3 * place, order)
        ot_onehot[:, here] = onehot_rows(types, type_count, slots)
        for comp in range(3):
            out_pos[index, comp : comp + 1, :] = xyz[comp]
    scale = [math.exp(-0.5 * k * k) for k in range(basis_count)]
    radial = [w_radial[k : k + 1, :] * scale[k] for k in range(basis_count)]
    radial_t = jnp.concatenate(radial + [jnp.zeros((channels - basis_count, channels), f32)], axis=0).T
    for k in range(basis_count):
        columns[k] = jnp.broadcast_to(radial_t[:, k : k + 1], (channels, slots))
    near = (ot_feat, ot_val, ot_carried_t, ot_onehot, ot_projected, ot_gains)
    value_t = w_value[...].astype(f32).T.astype(bf16)
    carry_values(slots, value_t, gain_columns(type_gain), identity(slots), near, slice(0, 6 * slots))

    def outer(place):
        return slice(place * third, (place + 1) * third)

    def pairs(place, s):
        cells = out_pos.at[place * 3 : place * 3 + 3]
        fill_pairs(basis_count, slots, cells, own_pos, place, -1, ot_terms[place], ot_weights[place], s)

    def sums(place, s):
        rows = chunk_of(s, chunk)
        summed[place][:, rows] = in_summed[place][:, rows] + dot_t(
            ot_carried_t[:, outer(place)], ot_weights[place][rows, :]
        )

    def epilogue(place):
        aggregate_t = None
        for k in range(basis_count):
            term = summed[place][:, k * slots : (k + 1) * slots] * columns[k]
            aggregate_t = term if aggregate_t is None else aggregate_t + term
        agg_half = aggregate_t.T.astype(bf16)
        cell = jnp.where(order[1] == 0, place, 1 - place)
        pre_act = dot(agg_half, w_out[...])
        sig = jax.nn.sigmoid(pre_act)
        center = in_feat[(3 * place + 1) * slots : (3 * place + 2) * slots, :]
        out_feat[0, cell] = (center.astype(f32) + pre_act * sig).astype(bf16)
        grad_pre = (
            cotangent[0, cell].astype(f32) * sig * (1.0 + pre_act * (1.0 - sig))
        ).astype(bf16)
        agg = dot_t(grad_pre, w_out[...]).astype(bf16).astype(f32)
        agg_t = agg.T
        for k in range(basis_count):
            here = slice(k * slots, (k + 1) * slots)
            scaled[place][here, :] = (agg * radial[k]).astype(bf16)
            scaled_t[place][:, here] = (agg_t * columns[k]).astype(bf16)
            product = agg_t * summed[place][:, here]
            products[:, here] = product if place == 0 else products[:, here] + product
        return dot(aggregate_t.astype(bf16), grad_pre)

    def weight_grads(place, s):
        rows = chunk_of(s, chunk)
        in_grad[place][rows, :] = dot_t(scaled[place][rows, :], in_val[...])
        ot_grad[place][rows, :] = dot_t(scaled[place][rows, :], ot_val[outer(place), :])

    def pulls(place, s):
        first, strip = strip_of(s)
        own_xyz = [own_pos[place, comp, strip, :] for comp in range(3)]
        total = [jnp.zeros((STRIP, slots), f32) for _ in range(3)]
        for block in range(9):
            inner = block < 6
            grad = (in_grad if inner else ot_grad)[place]
            terms = (in_terms if inner else ot_terms)[place]
            cells = in_pos if inner else out_pos
            cell = block if inner else place * 3 + block - 6
            index = block if inner else 6 + cell
            local = block if inner else block - 6
            there = slice(local * slots, (local + 1) * slots)

            def grad_of(k):
                rows = pl.ds(pl.multiple_of(first + k * slots, STRIP), STRIP)
                return grad[rows, there]

            step = terms[0, strip, there]
            value = grad_of(basis_count - 1)
            slope = None
            for k in range(basis_count - 2, -1, -1):
                slope = value if slope is None else value + step * slope
                value = grad_of(k) + step * value
            pull = terms[1, strip, there] * value + terms[2, strip, there] * slope
            for comp in range(3):
                force = pull * (cells[cell, comp : comp + 1, :] - own_xyz[comp])
                total[comp] = total[comp] + force
                pull_far[index, comp] += (force[0:8] + force[8:16]) + (force[16:24] + force[24:32])
        for comp in range(3):
            pull_own[place, comp, strip, :] = total[comp]

    def value_grads(s):
        rows = chunk_of(s, chunk)
        parts = [scaled_t[place][:, rows] for place in range(2)]
        in_back[...] += dot(parts[0], in_weights[0][rows, :]) + dot(parts[1], in_weights[1][rows, :])
        for place in range(2):
            ot_back[:, outer(place)] += dot(parts[place], ot_weights[place][rows, :])

    run = functools.partial
    pull_far[...] = jnp.zeros_like(pull_far)
    in_back[...] = jnp.zeros_like(in_back)
    ot_back[...] = jnp.zeros_like(ot_back)
    stage(strips, run(pairs, 0))
    stage(strips, run(sums, 0), run(pairs, 1))
    for s in range(strips):
        sums(1, s)
    wout = epilogue(0)
    for s in range(strips):
        weight_grads(0, s)
    wout = wout + epilogue(1)
    stage(strips, run(weight_grads, 1), run(pulls, 0))
    stage(strips, value_grads, run(pulls, 1))

    wvalue = ggain = None
    for back, feat, onehot, projected, gains in (
        (in_back, in_feat, in_onehot, in_projected, in_gains),
        (ot_back, ot_feat, ot_onehot, ot_projected, ot_gains),
    ):
        half = (back[...] * gains[...]).astype(bf16)
        hi, mid, _ = split3(back[...] * projected[...])
        wvalue_part = dot(half, feat[...])
        ggain_part = dot_t(hi, onehot[...]) + dot_t(mid, onehot[...])
        wvalue = wvalue_part if wvalue is None else wvalue + wvalue_part
        ggain = ggain_part if ggain is None else ggain + ggain_part
    ggain = jnp.concatenate([ggain, jnp.zeros((channels, slots - ggain.shape[1]), f32)], axis=1).T
    group = lax.broadcasted_iota(jnp.int32, (basis_count, basis_count * slots), 1) // slots
    mine = lax.broadcasted_iota(jnp.int32, (basis_count, basis_count * slots), 0)
    select = jnp.where(group == mine, 1.0, 0.0).astype(bf16)
    hi, mid, _ = split3(products[...])
    wradial = dot_t(select, hi) + dot_t(select, mid)
    wradial = jnp.concatenate([wradial[k : k + 1] * scale[k] for k in range(basis_count)], axis=0)
    pad = 2 * keep.shape[0] - 2 * channels - type_count - basis_count
    tail = [ggain[0:type_count], wradial] + ([jnp.zeros((pad, channels), f32)] if pad else [])
    full = jnp.concatenate([wvalue.T, wout] + tail, axis=0).astype(bf16)
    rows = keep.shape[0]
    whole[0] = full[0:rows]
    whole[1] = full[rows : 2 * rows]
    keep[...] = whole[order[0]]
    for ref in (pay_a, pay_b):
        ref[0:rows, :] = whole[1 - order[0]]
    force = float(basis_count - 1)
    size = slots + AUX
    for col in range(4):
        for row in range(3):
            inner = col in (1, 2)
            local = (col - 1) * 3 + row if inner else (0 if col == 0 else 3) + row
            back = (in_back if inner else ot_back)[:, local * slots : (local + 1) * slots]
            lines = []
            for comp in range(3):
                line = jnp.sum(pull_far[local if inner else 6 + local, comp], axis=0, keepdims=True)
                if row == 1 and inner:
                    line = line - jnp.sum(pull_own[col - 1, comp].T, axis=0, keepdims=True)
                lines.append(line * (force * HZ if comp == 2 else force))
            lines.append(jnp.zeros((AUX - 3, slots), f32))
            lines = jnp.concatenate(lines, axis=0)
            if row == 1:
                own_acc[col, 0:slots, :] = back
                own_acc[col, slots:size, :] = lines
                continue
            if inner:
                ref, base = (fold_a if row == 0 else fold_b), (col - 1) * size
            else:
                ref, base = (pay_a if row == 0 else pay_b), rows + (0 if col == 0 else size)
            ref[base : base + slots, :] = back.astype(bf16)
            ref[base + slots : base + size, :] = lines.astype(bf16)


def cell_grads(own, got_a, got_b, got, types_row, cotangent, w_value, type_gain):
    slots = cotangent.shape[0]
    total = own + (got_a.astype(f32) + got_b.astype(f32)) + got.astype(f32)
    gain = dot(gain_columns(type_gain), onehot_rows(types_row, type_gain.shape[0], slots))
    half = (total[0:slots] * gain).astype(bf16)
    feat = (cotangent.astype(f32) + dot(w_value[...], half).T).astype(bf16)
    return feat, total[slots : slots + 3]


def cells_kernel(
    order, own, got_a, got_b, far, near, types, cotangent, w_value, type_gain, grad_feat, grad_pos
):
    size = far.shape[0]
    for place in range(2):
        cell = jnp.where(order[1] == 0, place, 1 - place)
        here = slice(place * size, (place + 1) * size)
        got = far[...] if place == 0 else near[near.shape[0] - size :, :]
        feat, pos = cell_grads(
            own[place + 1], got_a[here, :], got_b[here, :], got, types[0, pl.ds(cell, 1), :],
            cotangent[0, cell], w_value, type_gain,
        )
        grad_feat[0, cell] = feat
        for comp in range(3):
            grad_pos[0, comp, pl.ds(cell, 1), :] = pos[comp : comp + 1]


def weights_kernel(order, mine, other, wvalue, wradial, ggain, wout):
    first = order[0] == 0
    low = jnp.where(first, mine[...], other[...])
    high = jnp.where(first, other[...], mine[...])
    total = jnp.concatenate([low, high], axis=0)
    base = 0
    for ref in (wvalue, wout, ggain, wradial):
        ref[...] = total[base : base + ref.shape[0]]
        base += ref.shape[0]


def edges(axis):
    count = lax.axis_size(axis)
    assert count % 2 == 0 and count > 2 and count & (count - 1) == 0
    even = [(i, i ^ 1) for i in range(count)]
    odd = [(i, (i + 1) % count if i % 2 else (i - 1) % count) for i in range(count)]
    return even, odd


def across(axis, step):
    return [(i, i ^ step) for i in range(lax.axis_size(axis))]


def add(a, b):
    return a.astype(f32) + b.astype(f32)


def on_device(
    features, positions, bead_types, cell_counts, w_value, w_radial, type_gain, w_out, cotangent
):
    row_count, col_count, slots, channels = features.shape
    basis_count, type_count = w_radial.shape[0], type_gain.shape[0]
    assert row_count == 1 and col_count == 2 and slots == channels == LANES
    assert 3 * type_count <= slots and type_count % 8 == 0 and basis_count == 8
    order = jnp.stack([lax.axis_index("gx") % 2, lax.axis_index("gy") % 2]).astype(jnp.int32)
    smem = pl.BlockSpec(memory_space=pltpu.SMEM)
    vmem = pl.BlockSpec(memory_space=pltpu.VMEM)
    x_even, x_odd = edges("gx")
    y_even, y_odd = edges("gy")
    size = slots + AUX
    inner, outer, tall = 6 * slots, 3 * slots, basis_count * slots
    rows = -(-(2 * channels + type_count + basis_count) // 32) * 16
    kinds = 3 * type_count
    shape = jax.ShapeDtypeStruct

    def call(kernel, mib, out_shape, arrays, scratch=()):
        return pl.pallas_call(
            kernel,
            out_shape=out_shape,
            in_specs=[smem] + [vmem] * len(arrays),
            out_specs=jax.tree.map(lambda _: vmem, out_shape),
            scratch_shapes=list(scratch),
            compiler_params=pltpu.CompilerParams(vmem_limit_bytes=mib * 2**20),
        )(order, *arrays)

    hbm = pl.BlockSpec(memory_space=pltpu.HBM)
    packed, bead_types, cotangent, w_value, w_radial, type_gain, w_out = pl.pallas_call(
        pack_kernel,
        out_shape=(
            shape((2, size, channels), bf16),
            *(shape(a.shape, a.dtype) for a in (bead_types, cotangent, w_value, w_radial, type_gain, w_out)),
        ),
        in_specs=[smem] + [hbm] * 9,
        out_specs=(vmem,) * 7,
        scratch_shapes=[
            pltpu.SMEM(cell_counts.shape, jnp.int32),
            pltpu.VMEM((row_count, 3, col_count, slots), f32),
            pltpu.SemaphoreType.DMA((10,)),
        ],
        compiler_params=pltpu.CompilerParams(vmem_limit_bytes=4 * 2**20),
        name="pack",
    )(
        order,
        *(
            pltpu.with_memory_space_constraint(a, pltpu.HBM)
            for a in (
                cell_counts, features, jnp.swapaxes(positions, 1, 2), bead_types, cotangent, w_value,
                w_radial, type_gain, w_out,
            )
        ),
    )
    row_b = lax.ppermute(packed, "gx", x_odd)
    row_a = lax.ppermute(packed, "gx", x_even)
    col_b = lax.ppermute(jnp.stack([row_a[0], packed[0], row_b[0]]), "gy", y_odd)
    col_a = lax.ppermute(jnp.stack([row_a[1], packed[1], row_b[1]]), "gy", y_even)
    early = call(
        functools.partial(early_kernel, basis_count), 8,
        (
            shape((6, 8, slots), f32),
            shape((2, 3, slots, slots), f32),
            shape((inner, channels), bf16),
            shape((inner, channels), bf16),
            shape((channels, inner), bf16),
            shape((kinds, inner), bf16),
            shape((channels, inner), f32),
            shape((channels, inner), f32),
        )
        + (shape((tall, inner), bf16),) * 2
        + (shape((3, slots, inner), f32),) * 2
        + (shape((channels, tall), f32),) * 2,
        (packed, row_a, row_b, w_value, type_gain),
    )
    out_feat, keep, pay_a, pay_b, fold_a, fold_b, own_acc = call(
        functools.partial(main_kernel, basis_count), 28,
        (
            shape(features.shape, bf16),
            shape((rows, channels), bf16),
            shape((rows + 2 * size, channels), bf16),
            shape((rows + 2 * size, channels), bf16),
            shape((2 * size, channels), bf16),
            shape((2 * size, channels), bf16),
            shape((4, size, slots), f32),
        ),
        (col_a, col_b, cotangent, w_value, w_radial, type_gain, w_out) + tuple(early),
        [
            pltpu.VMEM((6, 8, slots), f32),
            pltpu.VMEM((2 * outer, channels), bf16),
            pltpu.VMEM((2 * outer, channels), bf16),
            pltpu.VMEM((channels, 2 * outer), bf16),
            pltpu.VMEM((kinds, 2 * outer), bf16),
            pltpu.VMEM((channels, 2 * outer), f32),
            pltpu.VMEM((channels, 2 * outer), f32),
            pltpu.VMEM((basis_count, channels, slots), f32),
            pltpu.VMEM((channels, tall), f32),
            pltpu.VMEM((2, rows, channels), bf16),
        ]
        + [pltpu.VMEM((tall, outer), bf16)] * 2
        + [pltpu.VMEM((3, slots, outer), f32)] * 2
        + [pltpu.VMEM((channels, tall), f32)] * 2
        + [pltpu.VMEM((tall, channels), bf16)] * 2
        + [pltpu.VMEM((channels, tall), bf16)] * 2
        + [pltpu.VMEM((tall, inner), f32)] * 2
        + [pltpu.VMEM((tall, outer), f32)] * 2
        + [
            pltpu.VMEM((channels, inner), f32),
            pltpu.VMEM((channels, 2 * outer), f32),
            pltpu.VMEM((2, 3, slots, slots), f32),
            pltpu.VMEM((12, 3, 8, slots), f32),
        ],
    )
    got_b = lax.ppermute(pay_b, "gx", x_odd)
    got_a = lax.ppermute(pay_a, "gx", x_even)
    if len(x_even) == 4:
        other = lax.ppermute(keep, "gx", across("gx", 2))
        total = add(keep, got_a[:rows]) + add(other, got_b[:rows])
    else:
        total = add(keep, got_a[:rows])
        step = 2
        while step < len(x_even):
            part = total.astype(bf16)
            total = add(part, lax.ppermute(part, "gx", across("gx", step)))
            step *= 2
    part = total.astype(bf16)
    corner_b = own_acc[0] + add(got_a[rows : rows + size], got_b[rows : rows + size])
    corner_a = own_acc[3] + add(got_a[rows + size :], got_b[rows + size :])
    got = lax.ppermute(jnp.concatenate([part, corner_a.astype(bf16)]), "gy", y_even)
    far = lax.ppermute(corner_b.astype(bf16), "gy", y_odd)
    total = add(part, got[:rows])
    step = 2
    while step < len(y_even):
        part = total.astype(bf16)
        total = add(part, lax.ppermute(part, "gy", across("gy", step)))
        step *= 2
    half = lax.ppermute(total, "gx", x_even)
    fold_a, fold_b, got = lax.optimization_barrier((fold_a, fold_b, got))
    own_b = lax.ppermute(fold_b, "gx", x_odd)
    own_a = lax.ppermute(fold_a, "gx", x_even)
    grad_feat, grad_pos = call(
        cells_kernel, 4,
        (shape(features.shape, bf16), shape((row_count, 3, col_count, slots), f32)),
        (own_acc, own_a, own_b, far, got, bead_types, cotangent, w_value, type_gain),
    )
    wvalue, wradial, ggain, wout = call(
        weights_kernel, 4,
        (
            shape((channels, channels), f32),
            shape((basis_count, channels), f32),
            shape((type_count, channels), f32),
            shape((channels, channels), f32),
        ),
        (total, half),
    )
    return out_feat, grad_feat, jnp.swapaxes(grad_pos, 1, 2), wvalue, wradial, ggain, wout


def solution(mesh):
    cell = P(("frame", "gx"), "gy", None, None)

    return jax.shard_map(
        on_device,
        mesh=mesh,
        in_specs=(
            cell, cell, P(("frame", "gx"), "gy", None), P(("frame", "gx"), "gy"),
            P(), P(), P(), P(), cell,
        ),
        out_specs=(cell, cell, cell) + (P("frame", None),) * 4,
        check_vma=False,
    )
```

```python
import functools
import math

import jax
import jax.numpy as jnp
from jax import lax
from jax.experimental import pallas as pl
from jax.experimental.pallas import tpu as pltpu
from jax.sharding import PartitionSpec as P


HZ = 6
SOFTEN = 0.01
FAR = 1024.0
AUX = 16
STRIP = 32
LANES = 128
LOG2E = math.log2(math.e)


f32 = jnp.float32
bf16 = jnp.bfloat16


def split3(x):
    hi = x.astype(bf16)
    rest = x - hi.astype(f32)
    mid = rest.astype(bf16)
    low = (rest - mid.astype(f32)).astype(bf16)
    return hi, mid, low


def dot(a, b):
    return jnp.dot(a, b, preferred_element_type=f32)


def dot_t(a, b):
    return lax.dot_general(a, b, (((1,), (1,)), ((), ())), preferred_element_type=f32)


def identity(size):
    rows = lax.broadcasted_iota(jnp.int32, (size, size), 0)
    lanes = lax.broadcasted_iota(jnp.int32, (size, size), 1)
    return jnp.where(rows == lanes, 1.0, 0.0).astype(bf16)


def gain_columns(type_gain):
    parts = [part.astype(f32) for part in split3(type_gain[...])]
    count, channels = type_gain.shape
    rows = jnp.concatenate(parts + [jnp.zeros((channels - 3 * count, channels), f32)], axis=0)
    return rows.T[:, 0 : 3 * count].astype(bf16)


def onehot_rows(types_row, type_count, slots):
    rows = lax.broadcasted_iota(jnp.int32, (3 * type_count, slots), 0)
    hit = (rows == types_row) | (rows == types_row + type_count) | (rows == types_row + 2 * type_count)
    return jnp.where(hit, 1.0, 0.0).astype(bf16)


def pack_kernel(
    order, counts, feat, pos, types, cotangent, w_value, w_radial, type_gain, w_out,
    packed, cotangent_out, w_value_out, w_radial_out, type_gain_out, w_out_out,
    counts_here, pos_here, types_here, sems,
):
    slots = feat.shape[2]
    moves = [(counts, counts_here), (pos, pos_here), (types, types_here)]
    for place in range(2):
        cell = jnp.where(order[1] == 0, place, 1 - place)
        moves.append((feat.at[0, cell], packed.at[place, 0:slots, :]))
    moves += [
        (w_value, w_value_out), (type_gain, type_gain_out), (cotangent, cotangent_out),
        (w_radial, w_radial_out), (w_out, w_out_out),
    ]
    copies = [pltpu.make_async_copy(a, b, sems.at[i]) for i, (a, b) in enumerate(moves)]
    for copy in copies:
        copy.start()
    for copy in copies[:3]:
        copy.wait()
    for place in range(2):
        cell = jnp.where(order[1] == 0, place, 1 - place)
        lane = lax.broadcasted_iota(jnp.int32, (1, slots), 1)
        valid = lane < counts_here[0, cell]
        parts = [[], [], []]
        for comp in range(3):
            row = pos_here[0, comp, pl.ds(cell, 1), :]
            if comp == 2:
                row = row * float(HZ)
            row = jnp.where(valid, row, -FAR)
            for which, part in enumerate(split3(row)):
                parts[which].append(part.astype(f32))
        rows = parts[0] + parts[1] + parts[2]
        rows.append(types_here[0, pl.ds(cell, 1), :].astype(f32))
        rows.append(jnp.zeros((AUX - len(rows), slots), f32))
        packed[place, slots : slots + AUX, :] = jnp.concatenate(rows, axis=0).astype(bf16)
    for copy in copies[3:]:
        copy.wait()


def pair_terms(near_pos, index, own_xyz, is_self, first_row, basis_count):
    n1 = float(basis_count - 1)
    gamma = 0.5 * n1 * n1
    delta = [near_pos[index, comp : comp + 1, :] - own_xyz[comp] for comp in range(3)]
    dist_sq = delta[0] * delta[0] + delta[1] * delta[1] + delta[2] * delta[2]
    dist_sq = jnp.minimum(dist_sq, 1.0)
    inside = 1.0 - dist_sq
    radius_sq = dist_sq + SOFTEN
    inverse = lax.rsqrt(radius_sq)
    radius = radius_sq * inverse
    gauss = jnp.exp2(radius_sq * (-gamma * LOG2E))
    step = jnp.exp2(radius * (n1 * LOG2E))
    if is_self:
        rows = first_row + lax.broadcasted_iota(jnp.int32, gauss.shape, 0)
        lanes = lax.broadcasted_iota(jnp.int32, gauss.shape, 1)
        gauss = jnp.where(rows == lanes, 0.0, gauss)
    part = inside * gauss
    weight = inside * part
    value_factor = part * (inside * -n1 - 2.0 * n1 / gamma)
    slope_factor = weight * (inverse * step)
    return step, weight, value_factor, slope_factor


def near_cell(aux, row, col, order):
    sx = jnp.where(order[0] == 0, 1.0, -1.0).astype(f32)
    sy = jnp.where(order[1] == 0, 1.0, -1.0).astype(f32)
    aux = aux.astype(f32)
    xyz = aux[0:3] + aux[3:6] + aux[6:9]
    x = xyz[0:1] + sx * float(1 - row)
    y = xyz[1:2] + sy * float(col)
    return [x, y, xyz[2:3]], xyz[0:1] < -0.5 * FAR, aux[9:10].astype(jnp.int32)


def strip_of(s):
    first = pl.multiple_of(s * STRIP, STRIP)
    return first, pl.ds(first, STRIP)


def stage(count, *steps):
    def body(s, carry):
        for step in steps:
            step(s)
        return carry

    lax.fori_loop(0, count, body, 0)


def fill_pairs(basis_count, slots, near_pos, own_pos, place, self_block, terms, weights, s):
    first, strip = strip_of(s)
    own_xyz = [own_pos[place, comp, strip, :] for comp in range(3)]
    for block in range(weights.shape[1] // slots):
        there = slice(block * slots, (block + 1) * slots)
        step, weight, value_factor, slope_factor = pair_terms(
            near_pos, block, own_xyz, block == self_block, first, basis_count
        )
        terms[0, strip, there] = step
        terms[1, strip, there] = value_factor
        terms[2, strip, there] = slope_factor
        for k in range(basis_count):
            rows = pl.ds(pl.multiple_of(first + k * slots, STRIP), STRIP)
            weights[rows, there] = weight.astype(bf16)
            if k < basis_count - 1:
                weight = weight * step


def carry_values(slots, value_t, gain_t, eye, near, here):
    near_feat, near_val, carried_t, onehot, projected, gains = near
    proj = dot_t(value_t, near_feat[here, :])
    gain = dot(gain_t, onehot[:, here])
    projected[:, here] = proj
    gains[:, here] = gain
    carried = (proj * gain).astype(bf16)
    carried_t[:, here] = carried
    for first in range(here.start, here.stop, slots):
        there = slice(first - here.start, first - here.start + slots)
        near_val[first : first + slots, :] = dot_t(eye, carried[:, there]).astype(bf16)


def chunk_of(s, size):
    return pl.ds(pl.multiple_of(s * size, size), size)


def early_kernel(
    basis_count, order, own, row_a, row_b, w_value, type_gain,
    near_pos, own_pos, near_feat, near_val, carried_t, onehot, projected, gains,
    weights_b, weights_a, terms_b, terms_a, summed_b, summed_a,
):
    slots = near_feat.shape[1]
    strips = slots // STRIP
    chunk = basis_count * slots // strips
    weights, terms, summed = (weights_b, weights_a), (terms_b, terms_a), (summed_b, summed_a)
    for index in range(6):
        col, row = index // 3 + 1, index % 3
        ref = (row_a, own, row_b)[row]
        here = slice(index * slots, (index + 1) * slots)
        near_feat[here, :] = ref[col - 1, 0:slots, :]
        xyz, unused, types = near_cell(ref[col - 1, slots : slots + AUX, :], row, col, order)
        onehot[:, here] = onehot_rows(types, type_gain.shape[0], slots)
        for comp in range(3):
            near_pos[index, comp : comp + 1, :] = xyz[comp]
            if row == 1:
                line = jnp.where(unused, FAR, xyz[comp])
                own_pos[col - 1, comp] = jnp.broadcast_to(line, (slots, slots)).T
    near = (near_feat, near_val, carried_t, onehot, projected, gains)
    value_t = w_value[...].astype(f32).T.astype(bf16)
    carry_values(slots, value_t, gain_columns(type_gain), identity(slots), near, slice(0, 6 * slots))

    def sums(place, s):
        rows = chunk_of(s, chunk)
        summed[place][:, rows] = dot_t(carried_t[...], weights[place][rows, :])

    def pairs(place, s):
        fill_pairs(
            basis_count, slots, near_pos, own_pos, place, 3 * place + 1, terms[place], weights[place], s
        )

    run = functools.partial
    stage(strips, run(pairs, 0))
    stage(strips, run(sums, 0), run(pairs, 1))
    stage(strips, run(sums, 1))


def main_kernel(
    basis_count, order, col_a, col_b, cotangent, w_value, w_radial, type_gain, w_out,
    own_pos, in_feat, in_carried_t, in_onehot, in_projected, in_gains,
    in_weights_b, in_weights_a, in_summed_b, in_summed_a,
    out_feat, keep, pay_a, pay_b, fold_a, fold_b, own_acc,
    out_pos, ot_val, ot_terms_b, ot_terms_a, scaled_b, scaled_a,
    ot_feat, ot_carried_t, ot_onehot, ot_projected, ot_gains, columns, products, whole,
    ot_weights_b, ot_weights_a, summed_b, summed_a, scaled_tb, scaled_ta, in_back, ot_back,
):
    slots, channels = cotangent.shape[2], cotangent.shape[3]
    type_count = type_gain.shape[0]
    third = 3 * slots
    strips = slots // STRIP
    chunk = basis_count * slots // strips
    in_weights, ot_weights = (in_weights_b, in_weights_a), (ot_weights_b, ot_weights_a)
    ot_terms = (ot_terms_b, ot_terms_a)
    in_summed, summed = (in_summed_b, in_summed_a), (summed_b, summed_a)
    scaled, scaled_t = (scaled_b, scaled_a), (scaled_tb, scaled_ta)
    for index in range(6):
        place, row = index // 3, index % 3
        ref = (col_b, col_a)[place]
        here = slice(index * slots, (index + 1) * slots)
        ot_feat[here, :] = ref[row, 0:slots, :]
        xyz, _, types = near_cell(ref[row, slots : slots + AUX, :], row, 3 * place, order)
        ot_onehot[:, here] = onehot_rows(types, type_count, slots)
        for comp in range(3):
            out_pos[index, comp : comp + 1, :] = xyz[comp]
    scale = [math.exp(-0.5 * k * k) for k in range(basis_count)]
    radial = [w_radial[k : k + 1, :] * scale[k] for k in range(basis_count)]
    radial_t = jnp.concatenate(radial + [jnp.zeros((channels - basis_count, channels), f32)], axis=0).T
    for k in range(basis_count):
        columns[k] = jnp.broadcast_to(radial_t[:, k : k + 1], (channels, slots))
    near = (ot_feat, ot_val, ot_carried_t, ot_onehot, ot_projected, ot_gains)
    value_t = w_value[...].astype(f32).T.astype(bf16)
    carry_values(slots, value_t, gain_columns(type_gain), identity(slots), near, slice(0, 6 * slots))

    def outer(place):
        return slice(place * third, (place + 1) * third)

    def pairs(place, s):
        cells = out_pos.at[place * 3 : place * 3 + 3]
        fill_pairs(basis_count, slots, cells, own_pos, place, -1, ot_terms[place], ot_weights[place], s)

    def sums(place, s):
        rows = chunk_of(s, chunk)
        summed[place][:, rows] = in_summed[place][:, rows] + dot_t(
            ot_carried_t[:, outer(place)], ot_weights[place][rows, :]
        )

    def epilogue(place):
        aggregate_t = None
        for k in range(basis_count):
            term = summed[place][:, k * slots : (k + 1) * slots] * columns[k]
            aggregate_t = term if aggregate_t is None else aggregate_t + term
        agg_half = aggregate_t.T.astype(bf16)
        cell = jnp.where(order[1] == 0, place, 1 - place)
        pre_act = dot(agg_half, w_out[...])
        sig = jax.nn.sigmoid(pre_act)
        center = in_feat[(3 * place + 1) * slots : (3 * place + 2) * slots, :]
        out_feat[0, cell] = (center.astype(f32) + pre_act * sig).astype(bf16)
        grad_pre = (
            cotangent[0, cell].astype(f32) * sig * (1.0 + pre_act * (1.0 - sig))
        ).astype(bf16)
        agg = dot_t(grad_pre, w_out[...]).astype(bf16).astype(f32)
        agg_t = agg.T
        for k in range(basis_count):
            here = slice(k * slots, (k + 1) * slots)
            scaled[place][here, :] = (agg * radial[k]).astype(bf16)
            scaled_t[place][:, here] = (agg_t * columns[k]).astype(bf16)
            product = agg_t * summed[place][:, here]
            products[:, here] = product if place == 0 else products[:, here] + product
        return dot(aggregate_t.astype(bf16), grad_pre)

    def value_grads(place):
        inner = dot(scaled_t[place][...], in_weights[place][...])
        in_back[...] = inner if place == 0 else in_back[...] + inner
        ot_back[:, outer(place)] = dot(scaled_t[place][...], ot_weights[place][...])

    run = functools.partial
    stage(strips, run(pairs, 0))
    stage(strips, run(sums, 0), run(pairs, 1))
    for s in range(strips):
        sums(1, s)
    wout = epilogue(0)
    value_grads(0)
    wout = wout + epilogue(1)
    value_grads(1)

    wvalue = ggain = None
    for back, feat, onehot, projected, gains in (
        (in_back, in_feat, in_onehot, in_projected, in_gains),
        (ot_back, ot_feat, ot_onehot, ot_projected, ot_gains),
    ):
        half = (back[...] * gains[...]).astype(bf16)
        hi, mid, _ = split3(back[...] * projected[...])
        wvalue_part = dot(half, feat[...])
        ggain_part = dot_t(hi, onehot[...]) + dot_t(mid, onehot[...])
        wvalue = wvalue_part if wvalue is None else wvalue + wvalue_part
        ggain = ggain_part if ggain is None else ggain + ggain_part
    ggain = jnp.concatenate([ggain, jnp.zeros((channels, slots - ggain.shape[1]), f32)], axis=1).T
    group = lax.broadcasted_iota(jnp.int32, (basis_count, basis_count * slots), 1) // slots
    mine = lax.broadcasted_iota(jnp.int32, (basis_count, basis_count * slots), 0)
    select = jnp.where(group == mine, 1.0, 0.0).astype(bf16)
    hi, mid, _ = split3(products[...])
    wradial = dot_t(select, hi) + dot_t(select, mid)
    wradial = jnp.concatenate([wradial[k : k + 1] * scale[k] for k in range(basis_count)], axis=0)
    pad = 2 * keep.shape[0] - 2 * channels - type_count - basis_count
    tail = [ggain[0:type_count], wradial] + ([jnp.zeros((pad, channels), f32)] if pad else [])
    full = jnp.concatenate([wvalue.T, wout] + tail, axis=0).astype(bf16)
    rows = keep.shape[0]
    whole[0] = full[0:rows]
    whole[1] = full[rows : 2 * rows]
    keep[...] = whole[order[0]]
    for ref in (pay_a, pay_b):
        ref[0:rows, :] = whole[1 - order[0]]
    for col in range(4):
        for row in range(3):
            inner = col in (1, 2)
            local = (col - 1) * 3 + row if inner else (0 if col == 0 else 3) + row
            back = (in_back if inner else ot_back)[:, local * slots : (local + 1) * slots]
            if row == 1:
                own_acc[col] = back
            elif inner:
                ref = fold_a if row == 0 else fold_b
                ref[(col - 1) * slots : col * slots, :] = back.astype(bf16)
            else:
                ref = pay_a if row == 0 else pay_b
                base = rows + (0 if col == 0 else slots)
                ref[base : base + slots, :] = back.astype(bf16)


def pulls_kernel(
    basis_count, order, in_pos, own_pos, in_val, in_terms_b, in_terms_a, out_pos, ot_val,
    ot_terms_b, ot_terms_a, scaled_b, scaled_a,
    lines,
    in_grad_b, in_grad_a, ot_grad_b, ot_grad_a, pull_own, pull_far,
):
    slots = in_pos.shape[2]
    third = 3 * slots
    strips = slots // STRIP
    chunk = basis_count * slots // strips
    in_terms, ot_terms = (in_terms_b, in_terms_a), (ot_terms_b, ot_terms_a)
    scaled = (scaled_b, scaled_a)
    in_grad, ot_grad = (in_grad_b, in_grad_a), (ot_grad_b, ot_grad_a)

    def weight_grads(place, s):
        rows = chunk_of(s, chunk)
        in_grad[place][rows, :] = dot_t(scaled[place][rows, :], in_val[...])
        outer = slice(place * third, (place + 1) * third)
        ot_grad[place][rows, :] = dot_t(scaled[place][rows, :], ot_val[outer, :])

    def pulls(place, s):
        first, strip = strip_of(s)
        own_xyz = [own_pos[place, comp, strip, :] for comp in range(3)]
        total = [jnp.zeros((STRIP, slots), f32) for _ in range(3)]
        for block in range(9):
            inner = block < 6
            grad = (in_grad if inner else ot_grad)[place]
            terms = (in_terms if inner else ot_terms)[place]
            cells = in_pos if inner else out_pos
            cell = block if inner else place * 3 + block - 6
            index = block if inner else 6 + cell
            local = block if inner else block - 6
            there = slice(local * slots, (local + 1) * slots)

            def grad_of(k):
                rows = pl.ds(pl.multiple_of(first + k * slots, STRIP), STRIP)
                return grad[rows, there]

            step = terms[0, strip, there]
            value = grad_of(basis_count - 1)
            slope = None
            for k in range(basis_count - 2, -1, -1):
                slope = value if slope is None else value + step * slope
                value = grad_of(k) + step * value
            pull = terms[1, strip, there] * value + terms[2, strip, there] * slope
            for comp in range(3):
                force = pull * (cells[cell, comp : comp + 1, :] - own_xyz[comp])
                total[comp] = total[comp] + force
                pull_far[index, comp] += (force[0:8] + force[8:16]) + (force[16:24] + force[24:32])
        for comp in range(3):
            pull_own[place, comp, strip, :] = total[comp]

    run = functools.partial
    pull_far[...] = jnp.zeros_like(pull_far)
    for s in range(strips):
        weight_grads(0, s)
    stage(strips, run(weight_grads, 1), run(pulls, 0))
    stage(strips, run(pulls, 1))
    force = float(basis_count - 1)
    rows = []
    for col in range(4):
        for row in range(3):
            inner = col in (1, 2)
            local = (col - 1) * 3 + row if inner else 6 + (0 if col == 0 else 3) + row
            for comp in range(3):
                line = jnp.sum(pull_far[local, comp], axis=0, keepdims=True)
                if row == 1 and inner:
                    line = line - jnp.sum(pull_own[col - 1, comp].T, axis=0, keepdims=True)
                rows.append(line * (force * HZ if comp == 2 else force))
            rows.append(jnp.zeros((1, slots), f32))
        rows.append(jnp.zeros((4, slots), f32))
    lines[...] = jnp.concatenate(rows, axis=0)


def cells_kernel(
    order, own, got_a, got_b, far, near, lines, cotangent, w_value, gains, grad_feat, grad_pos
):
    slots = own.shape[2]
    for place in range(2):
        cell = jnp.where(order[1] == 0, place, 1 - place)
        here = slice(place * slots, (place + 1) * slots)
        got = far[0:slots, :] if place == 0 else near[near.shape[0] - AUX - slots : near.shape[0] - AUX, :]
        total = own[place + 1] + add(got_a[here, :], got_b[here, :]) + got.astype(f32)
        half = (total * gains[:, (3 * place + 1) * slots : (3 * place + 2) * slots]).astype(bf16)
        grad_feat[0, cell] = (cotangent[0, cell].astype(f32) + dot(w_value[...], half).T).astype(bf16)
        pos = lines[4 * place : 4 * place + 4, :]
        for comp in range(3):
            grad_pos[0, comp, pl.ds(cell, 1), :] = pos[comp : comp + 1]


def weights_kernel(order, mine, other, wvalue, wradial, ggain, wout):
    first = order[0] == 0
    low = jnp.where(first, mine[...], other[...])
    high = jnp.where(first, other[...], mine[...])
    total = jnp.concatenate([low, high], axis=0)
    base = 0
    for ref in (wvalue, wout, ggain, wradial):
        ref[...] = total[base : base + ref.shape[0]]
        base += ref.shape[0]


def edges(axis):
    count = lax.axis_size(axis)
    assert count % 2 == 0 and count > 2 and count & (count - 1) == 0
    even = [(i, i ^ 1) for i in range(count)]
    odd = [(i, (i + 1) % count if i % 2 else (i - 1) % count) for i in range(count)]
    return even, odd


def across(axis, step):
    return [(i, i ^ step) for i in range(lax.axis_size(axis))]


def add(a, b):
    return a.astype(f32) + b.astype(f32)


def on_device(
    features, positions, bead_types, cell_counts, w_value, w_radial, type_gain, w_out, cotangent
):
    row_count, col_count, slots, channels = features.shape
    basis_count, type_count = w_radial.shape[0], type_gain.shape[0]
    assert row_count == 1 and col_count == 2 and slots == channels == LANES
    assert 3 * type_count <= slots and type_count % 8 == 0 and basis_count == 8
    order = jnp.stack([lax.axis_index("gx") % 2, lax.axis_index("gy") % 2]).astype(jnp.int32)
    smem = pl.BlockSpec(memory_space=pltpu.SMEM)
    vmem = pl.BlockSpec(memory_space=pltpu.VMEM)
    x_even, x_odd = edges("gx")
    y_even, y_odd = edges("gy")
    size = slots + AUX
    inner, outer, tall = 6 * slots, 3 * slots, basis_count * slots
    rows = -(-(2 * channels + type_count + basis_count) // 32) * 16
    kinds = 3 * type_count
    shape = jax.ShapeDtypeStruct

    def call(kernel, mib, out_shape, arrays, scratch=()):
        return pl.pallas_call(
            kernel,
            out_shape=out_shape,
            in_specs=[smem] + [vmem] * len(arrays),
            out_specs=jax.tree.map(lambda _: vmem, out_shape),
            scratch_shapes=list(scratch),
            compiler_params=pltpu.CompilerParams(vmem_limit_bytes=mib * 2**20),
        )(order, *arrays)

    hbm = pl.BlockSpec(memory_space=pltpu.HBM)
    packed, *inputs = pl.pallas_call(
        pack_kernel,
        out_shape=(
            shape((2, size, channels), bf16),
            *(shape(a.shape, a.dtype) for a in (cotangent, w_value, w_radial, type_gain, w_out)),
        ),
        in_specs=[smem] + [hbm] * 9,
        out_specs=(vmem,) * 6,
        scratch_shapes=[
            pltpu.SMEM(cell_counts.shape, jnp.int32),
            pltpu.VMEM((row_count, 3, col_count, slots), f32),
            pltpu.VMEM(bead_types.shape, jnp.int32),
            pltpu.SemaphoreType.DMA((10,)),
        ],
        compiler_params=pltpu.CompilerParams(vmem_limit_bytes=4 * 2**20),
        name="pack",
    )(
        order,
        *(
            pltpu.with_memory_space_constraint(a, pltpu.HBM)
            for a in (
                cell_counts, features, jnp.swapaxes(positions, 1, 2), bead_types, cotangent, w_value,
                w_radial, type_gain, w_out,
            )
        ),
    )
    cotangent, w_value, w_radial, type_gain, w_out = inputs
    row_b = lax.ppermute(packed, "gx", x_odd)
    row_a = lax.ppermute(packed, "gx", x_even)
    col_b = lax.ppermute(jnp.stack([row_a[0], packed[0], row_b[0]]), "gy", y_odd)
    col_a = lax.ppermute(jnp.stack([row_a[1], packed[1], row_b[1]]), "gy", y_even)
    early = call(
        functools.partial(early_kernel, basis_count), 8,
        (
            shape((6, 8, slots), f32),
            shape((2, 3, slots, slots), f32),
            shape((inner, channels), bf16),
            shape((inner, channels), bf16),
            shape((channels, inner), bf16),
            shape((kinds, inner), bf16),
            shape((channels, inner), f32),
            shape((channels, inner), f32),
        )
        + (shape((tall, inner), bf16),) * 2
        + (shape((3, slots, inner), f32),) * 2
        + (shape((channels, tall), f32),) * 2,
        (packed, row_a, row_b, w_value, type_gain),
    )
    (
        in_pos, own_pos, in_feat, in_val, in_carried_t, in_onehot, in_projected, in_gains,
        in_weights_b, in_weights_a, in_terms_b, in_terms_a, in_summed_b, in_summed_a,
    ) = early
    (
        out_feat, keep, pay_a, pay_b, fold_a, fold_b, own_acc,
        out_pos, ot_val, ot_terms_b, ot_terms_a, scaled_b, scaled_a,
    ) = call(
        functools.partial(main_kernel, basis_count), 16,
        (
            shape(features.shape, bf16),
            shape((rows, channels), bf16),
            shape((rows + 2 * channels, slots), bf16),
            shape((rows + 2 * channels, slots), bf16),
            shape((2 * channels, slots), bf16),
            shape((2 * channels, slots), bf16),
            shape((4, channels, slots), f32),
            shape((6, 8, slots), f32),
            shape((2 * outer, channels), bf16),
        )
        + (shape((3, slots, outer), f32),) * 2
        + (shape((tall, channels), bf16),) * 2,
        (
            col_a, col_b, cotangent, w_value, w_radial, type_gain, w_out,
            own_pos, in_feat, in_carried_t, in_onehot, in_projected, in_gains,
            in_weights_b, in_weights_a, in_summed_b, in_summed_a,
        ),
        [
            pltpu.VMEM((2 * outer, channels), bf16),
            pltpu.VMEM((channels, 2 * outer), bf16),
            pltpu.VMEM((kinds, 2 * outer), bf16),
            pltpu.VMEM((channels, 2 * outer), f32),
            pltpu.VMEM((channels, 2 * outer), f32),
            pltpu.VMEM((basis_count, channels, slots), f32),
            pltpu.VMEM((channels, tall), f32),
            pltpu.VMEM((2, rows, channels), bf16),
        ]
        + [pltpu.VMEM((tall, outer), bf16)] * 2
        + [pltpu.VMEM((channels, tall), f32)] * 2
        + [pltpu.VMEM((channels, tall), bf16)] * 2
        + [pltpu.VMEM((channels, inner), f32), pltpu.VMEM((channels, 2 * outer), f32)],
    )
    got_b = lax.ppermute(pay_b, "gx", x_odd)
    got_a = lax.ppermute(pay_a, "gx", x_even)
    if len(x_even) == 4:
        other = lax.ppermute(keep, "gx", across("gx", 2))
        total = add(keep, got_a[:rows]) + add(other, got_b[:rows])
    else:
        total = add(keep, got_a[:rows])
        step = 2
        while step < len(x_even):
            part = total.astype(bf16)
            total = add(part, lax.ppermute(part, "gx", across("gx", step)))
            step *= 2
    lines = call(
        functools.partial(pulls_kernel, basis_count), 20, shape((4 * AUX, slots), f32),
        (
            in_pos, own_pos, in_val, in_terms_b, in_terms_a, out_pos, ot_val,
            ot_terms_b, ot_terms_a, scaled_b, scaled_a,
        ),
        [pltpu.VMEM((tall, inner), f32)] * 2
        + [pltpu.VMEM((tall, outer), f32)] * 2
        + [pltpu.VMEM((2, 3, slots, slots), f32), pltpu.VMEM((12, 3, 8, slots), f32)],
    )
    part = total.astype(bf16)
    corner_b = own_acc[0] + add(got_a[rows : rows + channels], got_b[rows : rows + channels])
    corner_a = own_acc[3] + add(got_a[rows + channels :], got_b[rows + channels :])
    sent = lines.astype(bf16)
    got = lax.ppermute(
        jnp.concatenate([part, corner_a.astype(bf16), sent[3 * AUX :]]), "gy", y_even
    )
    far = lax.ppermute(jnp.concatenate([corner_b.astype(bf16), sent[:AUX]]), "gy", y_odd)
    lines_here = lines[AUX : 3 * AUX]
    sent = lines_here.astype(bf16)
    own_b = lax.ppermute(jnp.concatenate([fold_b, sent]), "gx", x_odd)
    own_a = lax.ppermute(jnp.concatenate([fold_a, sent]), "gx", x_even)
    total = add(part, got[:rows])
    step = 2
    while step < len(y_even):
        part = total.astype(bf16)
        total = add(part, lax.ppermute(part, "gy", across("gy", step)))
        step *= 2
    sent = jnp.concatenate([far[channels:], got[rows + channels :]])
    more_b = lax.ppermute(sent, "gx", x_odd)
    more_a = lax.ppermute(sent, "gx", x_even)
    back_a = add(own_a[2 * channels :], more_a)
    back_b = add(own_b[2 * channels :], more_b)
    lines_here = lines_here + sent.astype(f32)
    pos = jnp.concatenate(
        [
            lines_here[base + 4 : base + 8] + (back_a[base : base + 4] + back_b[base + 8 : base + 12])
            for base in (0, AUX)
        ]
    )
    half = lax.ppermute(total, "gx", x_even)
    grad_feat, grad_pos = call(
        cells_kernel, 4,
        (shape(features.shape, bf16), shape((row_count, 3, col_count, slots), f32)),
        (own_acc, own_a, own_b, far, got, pos, cotangent, w_value, in_gains),
    )
    wvalue, wradial, ggain, wout = call(
        weights_kernel, 4,
        (
            shape((channels, channels), f32),
            shape((basis_count, channels), f32),
            shape((type_count, channels), f32),
            shape((channels, channels), f32),
        ),
        (total, half),
    )
    return out_feat, grad_feat, jnp.swapaxes(grad_pos, 1, 2), wvalue, wradial, ggain, wout


def solution(mesh):
    cell = P(("frame", "gx"), "gy", None, None)

    return jax.shard_map(
        on_device,
        mesh=mesh,
        in_specs=(
            cell, cell, P(("frame", "gx"), "gy", None), P(("frame", "gx"), "gy"),
            P(), P(), P(), P(), cell,
        ),
        out_specs=(cell, cell, cell) + (P("frame", None),) * 4,
        check_vma=False,
    )
```

```python
import functools
import math

import jax
import jax.numpy as jnp
from jax import lax
from jax.experimental import pallas as pl
from jax.experimental.pallas import tpu as pltpu
from jax.sharding import PartitionSpec as P


HZ = 6
SOFTEN = 0.01
FAR = 1024.0
AUX = 8
LINES = 16
STRIP = 32
LANES = 128
LOG2E = math.log2(math.e)


f32 = jnp.float32
bf16 = jnp.bfloat16


def split3(x):
    hi = x.astype(bf16)
    rest = x - hi.astype(f32)
    mid = rest.astype(bf16)
    low = (rest - mid.astype(f32)).astype(bf16)
    return hi, mid, low


def dot(a, b):
    return jnp.dot(a, b, preferred_element_type=f32)


def dot_t(a, b):
    return lax.dot_general(a, b, (((1,), (1,)), ((), ())), preferred_element_type=f32)


def identity(size):
    rows = lax.broadcasted_iota(jnp.int32, (size, size), 0)
    lanes = lax.broadcasted_iota(jnp.int32, (size, size), 1)
    return jnp.where(rows == lanes, 1.0, 0.0).astype(bf16)


def gain_columns(type_gain):
    parts = [part.astype(f32) for part in split3(type_gain[...])]
    count, channels = type_gain.shape
    rows = jnp.concatenate(parts + [jnp.zeros((channels - 3 * count, channels), f32)], axis=0)
    return rows.T[:, 0 : 3 * count].astype(bf16)


def onehot_rows(types_row, type_count, slots):
    rows = lax.broadcasted_iota(jnp.int32, (3 * type_count, slots), 0)
    hit = (rows == types_row) | (rows == types_row + type_count) | (rows == types_row + 2 * type_count)
    return jnp.where(hit, 1.0, 0.0).astype(bf16)


def pack_kernel(order, counts, feat, pos, types, packed, counts_here, pos_here, types_here, sems):
    slots = feat.shape[2]
    moves = [(counts, counts_here), (pos, pos_here), (types, types_here)]
    for place in range(2):
        cell = jnp.where(order[1] == 0, place, 1 - place)
        moves.append((feat.at[0, cell], packed.at[place, 0:slots, :]))
    copies = [pltpu.make_async_copy(a, b, sems.at[i]) for i, (a, b) in enumerate(moves)]
    for copy in copies:
        copy.start()
    for copy in copies[:3]:
        copy.wait()
    for place in range(2):
        cell = jnp.where(order[1] == 0, place, 1 - place)
        lane = lax.broadcasted_iota(jnp.int32, (1, slots), 1)
        valid = lane < counts_here[0, cell]
        parts = [[], []]
        for comp in range(3):
            row = pos_here[0, comp, pl.ds(cell, 1), :]
            if comp == 2:
                row = row * float(HZ)
            row = jnp.where(valid, row, -FAR)
            for which, part in enumerate(split3(row)[:2]):
                parts[which].append(part.astype(f32))
        rows = parts[0] + parts[1]
        rows.append(types_here[0, pl.ds(cell, 1), :].astype(f32))
        rows.append(jnp.zeros((AUX - len(rows), slots), f32))
        packed[place, slots : slots + AUX, :] = jnp.concatenate(rows, axis=0).astype(bf16)
    for copy in copies[3:]:
        copy.wait()


def load_kernel(*refs):
    sources, targets, sems = refs[:5], refs[5:10], refs[10]
    copies = [pltpu.make_async_copy(a, b, sems.at[i]) for i, (a, b) in enumerate(zip(sources, targets))]
    for copy in copies:
        copy.start()
    for copy in copies:
        copy.wait()


def pair_terms(near_pos, index, own_xyz, is_self, first_row, basis_count):
    n1 = float(basis_count - 1)
    gamma = 0.5 * n1 * n1
    delta = [near_pos[index, comp : comp + 1, :] - own_xyz[comp] for comp in range(3)]
    dist_sq = delta[0] * delta[0] + delta[1] * delta[1] + delta[2] * delta[2]
    dist_sq = jnp.minimum(dist_sq, 1.0)
    inside = 1.0 - dist_sq
    radius_sq = dist_sq + SOFTEN
    inverse = lax.rsqrt(radius_sq)
    radius = radius_sq * inverse
    gauss = jnp.exp2(radius_sq * (-gamma * LOG2E))
    step = jnp.exp2(radius * (n1 * LOG2E))
    if is_self:
        rows = first_row + lax.broadcasted_iota(jnp.int32, gauss.shape, 0)
        lanes = lax.broadcasted_iota(jnp.int32, gauss.shape, 1)
        gauss = jnp.where(rows == lanes, 0.0, gauss)
    part = inside * gauss
    weight = inside * part
    value_factor = part * (inside * -n1 - 2.0 * n1 / gamma)
    slope_factor = weight * (inverse * step)
    return step, weight, value_factor, slope_factor


def near_cell(aux, row, col, order):
    sx = jnp.where(order[0] == 0, 1.0, -1.0).astype(f32)
    sy = jnp.where(order[1] == 0, 1.0, -1.0).astype(f32)
    aux = aux.astype(f32)
    xyz = aux[0:3] + aux[3:6]
    x = xyz[0:1] + sx * float(1 - row)
    y = xyz[1:2] + sy * float(col)
    return [x, y, xyz[2:3]], xyz[0:1] < -0.5 * FAR, aux[6:7].astype(jnp.int32)


def strip_of(s):
    first = pl.multiple_of(s * STRIP, STRIP)
    return first, pl.ds(first, STRIP)


def stage(count, *steps):
    def body(s, carry):
        for step in steps:
            step(s)
        return carry

    lax.fori_loop(0, count, body, 0)


def fill_pairs(basis_count, slots, near_pos, own_pos, place, self_block, terms, weights, s):
    first, strip = strip_of(s)
    own_xyz = [own_pos[place, comp, strip, :] for comp in range(3)]
    for block in range(weights.shape[1] // slots):
        there = slice(block * slots, (block + 1) * slots)
        step, weight, value_factor, slope_factor = pair_terms(
            near_pos, block, own_xyz, block == self_block, first, basis_count
        )
        terms[0, strip, there] = step
        terms[1, strip, there] = value_factor
        terms[2, strip, there] = slope_factor
        for k in range(basis_count):
            rows = pl.ds(pl.multiple_of(first + k * slots, STRIP), STRIP)
            weights[rows, there] = weight.astype(bf16)
            if k < basis_count - 1:
                weight = weight * step


def carry_values(slots, value_t, gain_t, eye, near, here):
    near_feat, near_val, carried_t, onehot, projected, gains = near
    proj = dot_t(value_t, near_feat[here, :])
    gain = dot(gain_t, onehot[:, here])
    projected[:, here] = proj
    gains[:, here] = gain
    carried = (proj * gain).astype(bf16)
    carried_t[:, here] = carried
    for first in range(here.start, here.stop, slots):
        there = slice(first - here.start, first - here.start + slots)
        near_val[first : first + slots, :] = dot_t(eye, carried[:, there]).astype(bf16)


def chunk_of(s, size):
    return pl.ds(pl.multiple_of(s * size, size), size)


def early_kernel(
    basis_count, order, own, row_a, row_b, w_value, w_radial, type_gain,
    near_pos, own_pos, near_feat, near_val, carried_t, onehot, projected, gains,
    weights_b, weights_a, terms_b, terms_a, summed_b, summed_a, columns, value_t, gain_t,
):
    slots = near_feat.shape[1]
    strips = slots // STRIP
    chunk = basis_count * slots // strips
    weights, terms, summed = (weights_b, weights_a), (terms_b, terms_a), (summed_b, summed_a)
    for index in range(6):
        col, row = index // 3 + 1, index % 3
        ref = (row_a, own, row_b)[row]
        here = slice(index * slots, (index + 1) * slots)
        near_feat[here, :] = ref[col - 1, 0:slots, :]
        xyz, unused, types = near_cell(ref[col - 1, slots : slots + AUX, :], row, col, order)
        onehot[:, here] = onehot_rows(types, type_gain.shape[0], slots)
        for comp in range(3):
            near_pos[index, comp : comp + 1, :] = xyz[comp]
            if row == 1:
                line = jnp.where(unused, FAR, xyz[comp])
                own_pos[col - 1, comp] = jnp.broadcast_to(line, (slots, slots)).T
    near = (near_feat, near_val, carried_t, onehot, projected, gains)
    value_t[...] = w_value[...].astype(f32).T.astype(bf16)
    gain_t[...] = gain_columns(type_gain)
    carry_values(slots, value_t[...], gain_t[...], identity(slots), near, slice(0, 6 * slots))
    channels = w_value.shape[0]
    radial = [w_radial[k : k + 1, :] * math.exp(-0.5 * k * k) for k in range(basis_count)]
    radial_t = jnp.concatenate(radial + [jnp.zeros((channels - basis_count, channels), f32)], axis=0).T
    for k in range(basis_count):
        columns[k] = jnp.broadcast_to(radial_t[:, k : k + 1], (channels, slots))

    def sums(place, s):
        rows = chunk_of(s, chunk)
        summed[place][:, rows] = dot_t(carried_t[...], weights[place][rows, :])

    def pairs(place, s):
        fill_pairs(
            basis_count, slots, near_pos, own_pos, place, 3 * place + 1, terms[place], weights[place], s
        )

    run = functools.partial
    stage(strips, run(pairs, 0))
    stage(strips, run(sums, 0), run(pairs, 1))
    stage(strips, run(sums, 1))


def main_kernel(
    basis_count, order, col_a, col_b, cotangent, w_radial, w_out, columns, value_t, gain_t,
    own_pos, in_feat, in_carried_t, in_onehot, in_projected, in_gains,
    in_weights_b, in_weights_a, in_summed_b, in_summed_a,
    out_here, keep, pay_a, pay_b, fold_a, fold_b, own_acc,
    out_pos, ot_val, ot_terms_b, ot_terms_a, grad_agg,
    ot_feat, ot_carried_t, ot_onehot, ot_projected, ot_gains, products, whole,
    ot_weights_b, ot_weights_a, summed_b, summed_a, scaled_tb, scaled_ta, in_back, ot_back,
):
    slots, channels = cotangent.shape[2], cotangent.shape[3]
    type_count = gain_t.shape[1] // 3
    third = 3 * slots
    strips = slots // STRIP
    chunk = basis_count * slots // strips
    in_weights, ot_weights = (in_weights_b, in_weights_a), (ot_weights_b, ot_weights_a)
    ot_terms = (ot_terms_b, ot_terms_a)
    in_summed, summed = (in_summed_b, in_summed_a), (summed_b, summed_a)
    scaled_t = (scaled_tb, scaled_ta)
    for index in range(6):
        place, row = index // 3, index % 3
        ref = (col_b, col_a)[place]
        here = slice(index * slots, (index + 1) * slots)
        ot_feat[here, :] = ref[row, 0:slots, :]
        xyz, _, types = near_cell(ref[row, slots : slots + AUX, :], row, 3 * place, order)
        ot_onehot[:, here] = onehot_rows(types, type_count, slots)
        for comp in range(3):
            out_pos[index, comp : comp + 1, :] = xyz[comp]
    scale = [math.exp(-0.5 * k * k) for k in range(basis_count)]
    near = (ot_feat, ot_val, ot_carried_t, ot_onehot, ot_projected, ot_gains)
    carry_values(slots, value_t[...], gain_t[...], identity(slots), near, slice(0, 6 * slots))

    def outer(place):
        return slice(place * third, (place + 1) * third)

    def pairs(place, s):
        cells = out_pos.at[place * 3 : place * 3 + 3]
        fill_pairs(basis_count, slots, cells, own_pos, place, -1, ot_terms[place], ot_weights[place], s)

    def sums(place, s):
        rows = chunk_of(s, chunk)
        summed[place][:, rows] = in_summed[place][:, rows] + dot_t(
            ot_carried_t[:, outer(place)], ot_weights[place][rows, :]
        )

    def epilogue(place):
        aggregate_t = None
        for k in range(basis_count):
            term = summed[place][:, k * slots : (k + 1) * slots] * columns[k]
            aggregate_t = term if aggregate_t is None else aggregate_t + term
        agg_half = aggregate_t.T.astype(bf16)
        cell = jnp.where(order[1] == 0, place, 1 - place)
        pre_act = dot(agg_half, w_out[...])
        sig = jax.nn.sigmoid(pre_act)
        center = in_feat[(3 * place + 1) * slots : (3 * place + 2) * slots, :]
        out_here[place] = (center.astype(f32) + pre_act * sig).astype(bf16)
        grad_pre = (
            cotangent[0, cell].astype(f32) * sig * (1.0 + pre_act * (1.0 - sig))
        ).astype(bf16)
        agg_half = dot_t(grad_pre, w_out[...]).astype(bf16)
        grad_agg[place] = agg_half
        agg_t = agg_half.astype(f32).T
        for k in range(basis_count):
            here = slice(k * slots, (k + 1) * slots)
            scaled_t[place][:, here] = (agg_t * columns[k]).astype(bf16)
            product = agg_t * summed[place][:, here]
            products[:, here] = product if place == 0 else products[:, here] + product
        return dot(aggregate_t.astype(bf16), grad_pre)

    def value_grads(place):
        inner = dot(scaled_t[place][...], in_weights[place][...])
        in_back[...] = inner if place == 0 else in_back[...] + inner
        ot_back[:, outer(place)] = dot(scaled_t[place][...], ot_weights[place][...])

    run = functools.partial
    stage(strips, run(pairs, 0))
    stage(strips, run(sums, 0), run(pairs, 1))
    for s in range(strips):
        sums(1, s)
    wout = epilogue(0)
    value_grads(0)
    wout = wout + epilogue(1)
    value_grads(1)

    wvalue = ggain = None
    for back, feat, onehot, projected, gains in (
        (in_back, in_feat, in_onehot, in_projected, in_gains),
        (ot_back, ot_feat, ot_onehot, ot_projected, ot_gains),
    ):
        half = (back[...] * gains[...]).astype(bf16)
        wvalue_part = dot(half, feat[...])
        ggain_part = dot_t((back[...] * projected[...]).astype(bf16), onehot[0:type_count, :])
        wvalue = wvalue_part if wvalue is None else wvalue + wvalue_part
        ggain = ggain_part if ggain is None else ggain + ggain_part
    ggain = jnp.concatenate([ggain, jnp.zeros((channels, slots - ggain.shape[1]), f32)], axis=1).T
    group = lax.broadcasted_iota(jnp.int32, (basis_count, basis_count * slots), 1) // slots
    mine = lax.broadcasted_iota(jnp.int32, (basis_count, basis_count * slots), 0)
    select = jnp.where(group == mine, 1.0, 0.0).astype(bf16)
    wradial = dot_t(select, products[...].astype(bf16))
    wradial = jnp.concatenate([wradial[k : k + 1] * scale[k] for k in range(basis_count)], axis=0)
    pad = 2 * keep.shape[0] - 2 * channels - type_count - basis_count
    tail = [ggain[0:type_count], wradial] + ([jnp.zeros((pad, channels), f32)] if pad else [])
    full = jnp.concatenate([wvalue.T, wout] + tail, axis=0).astype(bf16)
    rows = keep.shape[0]
    whole[0] = full[0:rows]
    whole[1] = full[rows : 2 * rows]
    keep[...] = whole[order[0]]
    for ref in (pay_a, pay_b):
        ref[0:rows, :] = whole[1 - order[0]]
    for col in range(4):
        for row in range(3):
            inner = col in (1, 2)
            local = (col - 1) * 3 + row if inner else (0 if col == 0 else 3) + row
            back = (in_back if inner else ot_back)[:, local * slots : (local + 1) * slots]
            if row == 1:
                own_acc[col] = back
            elif inner:
                ref = fold_a if row == 0 else fold_b
                ref[(col - 1) * slots : col * slots, :] = back.astype(bf16)
            else:
                ref = pay_a if row == 0 else pay_b
                base = rows + (0 if col == 0 else slots)
                ref[base : base + slots, :] = back.astype(bf16)


def pulls_kernel(
    basis_count, order, in_pos, own_pos, in_val, in_terms_b, in_terms_a, out_pos, ot_val,
    ot_terms_b, ot_terms_a, grad_agg, w_radial,
    lines,
    scaled_b, scaled_a, in_grad_b, in_grad_a, ot_grad_b, ot_grad_a, pull_own, pull_far,
):
    slots = in_pos.shape[2]
    third = 3 * slots
    strips = slots // STRIP
    chunk = basis_count * slots // strips
    in_terms, ot_terms = (in_terms_b, in_terms_a), (ot_terms_b, ot_terms_a)
    scaled = (scaled_b, scaled_a)
    in_grad, ot_grad = (in_grad_b, in_grad_a), (ot_grad_b, ot_grad_a)

    def weight_grads(place, s):
        rows = chunk_of(s, chunk)
        in_grad[place][rows, :] = dot_t(scaled[place][rows, :], in_val[...])
        outer = slice(place * third, (place + 1) * third)
        ot_grad[place][rows, :] = dot_t(scaled[place][rows, :], ot_val[outer, :])

    def pulls(place, s):
        first, strip = strip_of(s)
        own_xyz = [own_pos[place, comp, strip, :] for comp in range(3)]
        total = [jnp.zeros((STRIP, slots), f32) for _ in range(3)]
        for block in range(9):
            inner = block < 6
            grad = (in_grad if inner else ot_grad)[place]
            terms = (in_terms if inner else ot_terms)[place]
            cells = in_pos if inner else out_pos
            cell = block if inner else place * 3 + block - 6
            index = block if inner else 6 + cell
            local = block if inner else block - 6
            there = slice(local * slots, (local + 1) * slots)

            def grad_of(k):
                rows = pl.ds(pl.multiple_of(first + k * slots, STRIP), STRIP)
                return grad[rows, there]

            step = terms[0, strip, there]
            value = grad_of(basis_count - 1)
            slope = None
            for k in range(basis_count - 2, -1, -1):
                slope = value if slope is None else value + step * slope
                value = grad_of(k) + step * value
            pull = terms[1, strip, there] * value + terms[2, strip, there] * slope
            for comp in range(3):
                force = pull * (cells[cell, comp : comp + 1, :] - own_xyz[comp])
                total[comp] = total[comp] + force
                pull_far[index, comp] += (force[0:8] + force[8:16]) + (force[16:24] + force[24:32])
        for comp in range(3):
            pull_own[place, comp, strip, :] = total[comp]

    run = functools.partial
    pull_far[...] = jnp.zeros_like(pull_far)
    for place in range(2):
        agg = grad_agg[place].astype(f32)
        for k in range(basis_count):
            factor = w_radial[k : k + 1, :] * math.exp(-0.5 * k * k)
            scaled[place][k * slots : (k + 1) * slots, :] = (agg * factor).astype(bf16)
        if place == 0:
            for s in range(strips):
                weight_grads(0, s)
    stage(strips, run(weight_grads, 1), run(pulls, 0))
    stage(strips, run(pulls, 1))
    force = float(basis_count - 1)
    rows = []
    for col in range(4):
        for row in range(3):
            inner = col in (1, 2)
            local = (col - 1) * 3 + row if inner else 6 + (0 if col == 0 else 3) + row
            for comp in range(3):
                line = jnp.sum(pull_far[local, comp], axis=0, keepdims=True)
                if row == 1 and inner:
                    line = line - jnp.sum(pull_own[col - 1, comp].T, axis=0, keepdims=True)
                rows.append(line * (force * HZ if comp == 2 else force))
            rows.append(jnp.zeros((1, slots), f32))
        rows.append(jnp.zeros((4, slots), f32))
    lines[...] = jnp.concatenate(rows, axis=0)


def cells_kernel(
    order, own, got_a, got_b, far, near, lines, cotangent, w_value, gains, grad_feat, grad_pos
):
    slots = own.shape[2]
    for place in range(2):
        cell = jnp.where(order[1] == 0, place, 1 - place)
        here = slice(place * slots, (place + 1) * slots)
        got = far[0:slots, :] if place == 0 else near[near.shape[0] - LINES - slots : near.shape[0] - LINES, :]
        total = own[place + 1] + add(got_a[here, :], got_b[here, :]) + got.astype(f32)
        half = (total * gains[:, (3 * place + 1) * slots : (3 * place + 2) * slots]).astype(bf16)
        grad_feat[0, cell] = (cotangent[0, cell].astype(f32) + dot(w_value[...], half).T).astype(bf16)
        pos = lines[4 * place : 4 * place + 4, :]
        for comp in range(3):
            grad_pos[0, comp, pl.ds(cell, 1), :] = pos[comp : comp + 1]


def emit_kernel(order, out_here, out_feat):
    for place in range(2):
        out_feat[0, jnp.where(order[1] == 0, place, 1 - place)] = out_here[place]


def finish_kernel(order, mine, other, feat, pos, grad_feat, grad_pos, wvalue, wradial, ggain, wout):
    grad_feat[...] = feat[...]
    grad_pos[...] = pos[...]
    first = order[0] == 0
    low = jnp.where(first, mine[...], other[...])
    high = jnp.where(first, other[...], mine[...])
    total = jnp.concatenate([low, high], axis=0)
    base = 0
    for ref in (wvalue, wout, ggain, wradial):
        ref[...] = total[base : base + ref.shape[0]]
        base += ref.shape[0]


def edges(axis):
    count = lax.axis_size(axis)
    assert count % 2 == 0 and count > 2 and count & (count - 1) == 0
    even = [(i, i ^ 1) for i in range(count)]
    odd = [(i, (i + 1) % count if i % 2 else (i - 1) % count) for i in range(count)]
    return even, odd


def across(axis, step):
    return [(i, i ^ step) for i in range(lax.axis_size(axis))]


def add(a, b):
    return a.astype(f32) + b.astype(f32)


def on_device(
    features, positions, bead_types, cell_counts, w_value, w_radial, type_gain, w_out, cotangent
):
    row_count, col_count, slots, channels = features.shape
    basis_count, type_count = w_radial.shape[0], type_gain.shape[0]
    assert row_count == 1 and col_count == 2 and slots == channels == LANES
    assert 3 * type_count <= slots and type_count % 8 == 0 and basis_count == 8
    order = jnp.stack([lax.axis_index("gx") % 2, lax.axis_index("gy") % 2]).astype(jnp.int32)
    smem = pl.BlockSpec(memory_space=pltpu.SMEM)
    vmem = pl.BlockSpec(memory_space=pltpu.VMEM)
    x_even, x_odd = edges("gx")
    y_even, y_odd = edges("gy")
    size = slots + AUX
    inner, outer, tall = 6 * slots, 3 * slots, basis_count * slots
    rows = -(-(2 * channels + type_count + basis_count) // 32) * 16
    kinds = 3 * type_count
    shape = jax.ShapeDtypeStruct

    def call(kernel, mib, out_shape, arrays, scratch=()):
        return pl.pallas_call(
            kernel,
            out_shape=out_shape,
            in_specs=[smem] + [vmem] * len(arrays),
            out_specs=jax.tree.map(lambda _: vmem, out_shape),
            scratch_shapes=list(scratch),
            compiler_params=pltpu.CompilerParams(vmem_limit_bytes=mib * 2**20),
        )(order, *arrays)

    hbm = pl.BlockSpec(memory_space=pltpu.HBM)
    small = pltpu.CompilerParams(vmem_limit_bytes=4 * 2**20)

    def in_hbm(*arrays):
        return [pltpu.with_memory_space_constraint(a, pltpu.HBM) for a in arrays]

    packed = pl.pallas_call(
        pack_kernel,
        out_shape=shape((2, size, channels), bf16),
        in_specs=[smem] + [hbm] * 4,
        out_specs=vmem,
        scratch_shapes=[
            pltpu.SMEM(cell_counts.shape, jnp.int32),
            pltpu.VMEM((row_count, 3, col_count, slots), f32),
            pltpu.VMEM(bead_types.shape, jnp.int32),
            pltpu.SemaphoreType.DMA((5,)),
        ],
        compiler_params=small,
        name="pack",
    )(order, *in_hbm(cell_counts, features, jnp.swapaxes(positions, 1, 2), bead_types))
    later = (cotangent, w_value, w_radial, type_gain, w_out)
    cotangent, w_value, w_radial, type_gain, w_out = pl.pallas_call(
        load_kernel,
        out_shape=tuple(shape(a.shape, a.dtype) for a in later),
        in_specs=[hbm] * 5,
        out_specs=(vmem,) * 5,
        scratch_shapes=[pltpu.SemaphoreType.DMA((5,))],
        compiler_params=small,
        name="load",
    )(*in_hbm(*later))
    row_b = lax.ppermute(packed, "gx", x_odd)
    row_a = lax.ppermute(packed, "gx", x_even)
    col_b = lax.ppermute(jnp.stack([row_a[0], packed[0], row_b[0]]), "gy", y_odd)
    col_a = lax.ppermute(jnp.stack([row_a[1], packed[1], row_b[1]]), "gy", y_even)
    early = call(
        functools.partial(early_kernel, basis_count), 8,
        (
            shape((6, 8, slots), f32),
            shape((2, 3, slots, slots), f32),
            shape((inner, channels), bf16),
            shape((inner, channels), bf16),
            shape((channels, inner), bf16),
            shape((kinds, inner), bf16),
            shape((channels, inner), f32),
            shape((channels, inner), f32),
        )
        + (shape((tall, inner), bf16),) * 2
        + (shape((3, slots, inner), f32),) * 2
        + (shape((channels, tall), f32),) * 2
        + (
            shape((basis_count, channels, slots), f32),
            shape((channels, channels), bf16),
            shape((channels, kinds), bf16),
        ),
        (packed, row_a, row_b, w_value, w_radial, type_gain),
    )
    (
        in_pos, own_pos, in_feat, in_val, in_carried_t, in_onehot, in_projected, in_gains,
        in_weights_b, in_weights_a, in_terms_b, in_terms_a, in_summed_b, in_summed_a,
        columns, value_t, gain_t,
    ) = early
    (
        out_here, keep, pay_a, pay_b, fold_a, fold_b, own_acc,
        out_pos, ot_val, ot_terms_b, ot_terms_a, grad_agg,
    ) = call(
        functools.partial(main_kernel, basis_count), 16,
        (
            shape((2, slots, channels), bf16),
            shape((rows, channels), bf16),
            shape((rows + 2 * channels, slots), bf16),
            shape((rows + 2 * channels, slots), bf16),
            shape((2 * channels, slots), bf16),
            shape((2 * channels, slots), bf16),
            shape((4, channels, slots), f32),
            shape((6, 8, slots), f32),
            shape((2 * outer, channels), bf16),
        )
        + (shape((3, slots, outer), f32),) * 2
        + (shape((2, slots, channels), bf16),),
        (
            col_a, col_b, cotangent, w_radial, w_out, columns, value_t, gain_t,
            own_pos, in_feat, in_carried_t, in_onehot, in_projected, in_gains,
            in_weights_b, in_weights_a, in_summed_b, in_summed_a,
        ),
        [
            pltpu.VMEM((2 * outer, channels), bf16),
            pltpu.VMEM((channels, 2 * outer), bf16),
            pltpu.VMEM((kinds, 2 * outer), bf16),
            pltpu.VMEM((channels, 2 * outer), f32),
            pltpu.VMEM((channels, 2 * outer), f32),
            pltpu.VMEM((channels, tall), f32),
            pltpu.VMEM((2, rows, channels), bf16),
        ]
        + [pltpu.VMEM((tall, outer), bf16)] * 2
        + [pltpu.VMEM((channels, tall), f32)] * 2
        + [pltpu.VMEM((channels, tall), bf16)] * 2
        + [pltpu.VMEM((channels, inner), f32), pltpu.VMEM((channels, 2 * outer), f32)],
    )
    got_b = lax.ppermute(pay_b, "gx", x_odd)
    got_a = lax.ppermute(pay_a, "gx", x_even)
    if len(x_even) == 4:
        other = lax.ppermute(keep, "gx", across("gx", 2))
        total = add(keep, got_a[:rows]) + add(other, got_b[:rows])
    else:
        total = add(keep, got_a[:rows])
        step = 2
        while step < len(x_even):
            part = total.astype(bf16)
            total = add(part, lax.ppermute(part, "gx", across("gx", step)))
            step *= 2
    lines = call(
        functools.partial(pulls_kernel, basis_count), 20, shape((4 * LINES, slots), f32),
        (
            in_pos, own_pos, in_val, in_terms_b, in_terms_a, out_pos, ot_val,
            ot_terms_b, ot_terms_a, grad_agg, w_radial,
        ),
        [pltpu.VMEM((tall, channels), bf16)] * 2
        + [pltpu.VMEM((tall, inner), f32)] * 2
        + [pltpu.VMEM((tall, outer), f32)] * 2
        + [pltpu.VMEM((2, 3, slots, slots), f32), pltpu.VMEM((12, 3, 8, slots), f32)],
    )
    part = total.astype(bf16)
    corner_b = own_acc[0] + add(got_a[rows : rows + channels], got_b[rows : rows + channels])
    corner_a = own_acc[3] + add(got_a[rows + channels :], got_b[rows + channels :])
    sent = lines.astype(bf16)
    got = lax.ppermute(
        jnp.concatenate([part, corner_a.astype(bf16), sent[3 * LINES :]]), "gy", y_even
    )
    far = lax.ppermute(jnp.concatenate([corner_b.astype(bf16), sent[:LINES]]), "gy", y_odd)
    lines_here = lines[LINES : 3 * LINES]
    sent = lines_here.astype(bf16)
    own_b = lax.ppermute(jnp.concatenate([fold_b, sent]), "gx", x_odd)
    own_a = lax.ppermute(jnp.concatenate([fold_a, sent]), "gx", x_even)
    total = add(part, got[:rows])
    step = 2
    while step < len(y_even):
        part = total.astype(bf16)
        got_far = lax.ppermute(part, "gy", across("gy", step))
        total = add(part, got_far)
        step *= 2
    sent = jnp.concatenate([far[channels:], got[rows + channels :]])
    more_b = lax.ppermute(sent, "gx", x_odd)
    more_a = lax.ppermute(sent, "gx", x_even)
    back_a = add(own_a[2 * channels :], more_a)
    back_b = add(own_b[2 * channels :], more_b)
    lines_here = lines_here + sent.astype(f32)
    pos = jnp.concatenate(
        [
            lines_here[base + 4 : base + 8] + (back_a[base : base + 4] + back_b[base + 8 : base + 12])
            for base in (0, LINES)
        ]
    )
    out_feat = call(emit_kernel, 4, shape(features.shape, bf16), (out_here,))
    half = lax.ppermute(total, "gx", x_even)
    grad_feat, grad_pos = call(
        cells_kernel, 4,
        (shape(features.shape, bf16), shape((row_count, 3, col_count, slots), f32)),
        (own_acc, own_a, own_b, far, got, pos, cotangent, w_value, in_gains),
    )
    grad_feat, grad_pos, wvalue, wradial, ggain, wout = call(
        finish_kernel, 4,
        (
            shape(grad_feat.shape, bf16),
            shape(grad_pos.shape, f32),
            shape((channels, channels), f32),
            shape((basis_count, channels), f32),
            shape((type_count, channels), f32),
            shape((channels, channels), f32),
        ),
        (total, half, grad_feat, grad_pos),
    )
    return out_feat, grad_feat, jnp.swapaxes(grad_pos, 1, 2), wvalue, wradial, ggain, wout


def solution(mesh):
    cell = P(("frame", "gx"), "gy", None, None)

    return jax.shard_map(
        on_device,
        mesh=mesh,
        in_specs=(
            cell, cell, P(("frame", "gx"), "gy", None), P(("frame", "gx"), "gy"),
            P(), P(), P(), P(), cell,
        ),
        out_specs=(cell, cell, cell) + (P("frame", None),) * 4,
        check_vma=False,
    )
```

```python
import functools
import math

import jax
import jax.numpy as jnp
from jax import lax
from jax.experimental import pallas as pl
from jax.experimental.pallas import tpu as pltpu
from jax.sharding import PartitionSpec as P


HZ = 6
SOFTEN = 0.01
FAR = 1024.0
AUX = 8
LINES = 16
STRIP = 32
LANES = 128
LOG2E = math.log2(math.e)


f32 = jnp.float32
bf16 = jnp.bfloat16


def split3(x):
    hi = x.astype(bf16)
    rest = x - hi.astype(f32)
    mid = rest.astype(bf16)
    low = (rest - mid.astype(f32)).astype(bf16)
    return hi, mid, low


def dot(a, b):
    return jnp.dot(a, b, preferred_element_type=f32)


def dot_t(a, b):
    return lax.dot_general(a, b, (((1,), (1,)), ((), ())), preferred_element_type=f32)


def identity(size):
    rows = lax.broadcasted_iota(jnp.int32, (size, size), 0)
    lanes = lax.broadcasted_iota(jnp.int32, (size, size), 1)
    return jnp.where(rows == lanes, 1.0, 0.0).astype(bf16)


def gain_columns(type_gain):
    parts = [part.astype(f32) for part in split3(type_gain[...])]
    count, channels = type_gain.shape
    rows = jnp.concatenate(parts + [jnp.zeros((channels - 3 * count, channels), f32)], axis=0)
    return rows.T[:, 0 : 3 * count].astype(bf16)


def onehot_rows(types_row, type_count, slots):
    rows = lax.broadcasted_iota(jnp.int32, (3 * type_count, slots), 0)
    hit = (rows == types_row) | (rows == types_row + type_count) | (rows == types_row + 2 * type_count)
    return jnp.where(hit, 1.0, 0.0).astype(bf16)


def pack_kernel(order, counts, feat, pos, types, packed, counts_here, pos_here, types_here, sems):
    slots = feat.shape[2]
    moves = [(counts, counts_here), (pos, pos_here), (types, types_here)]
    for place in range(2):
        cell = jnp.where(order[1] == 0, place, 1 - place)
        moves.append((feat.at[0, cell], packed.at[place, 0:slots, :]))
    copies = [pltpu.make_async_copy(a, b, sems.at[i]) for i, (a, b) in enumerate(moves)]
    for copy in copies:
        copy.start()
    for copy in copies[:3]:
        copy.wait()
    for place in range(2):
        cell = jnp.where(order[1] == 0, place, 1 - place)
        lane = lax.broadcasted_iota(jnp.int32, (1, slots), 1)
        valid = lane < counts_here[0, cell]
        parts = [[], []]
        for comp in range(3):
            row = pos_here[0, comp, pl.ds(cell, 1), :]
            if comp == 2:
                row = row * float(HZ)
            row = jnp.where(valid, row, -FAR)
            for which, part in enumerate(split3(row)[:2]):
                parts[which].append(part.astype(f32))
        rows = parts[0] + parts[1]
        rows.append(types_here[0, pl.ds(cell, 1), :].astype(f32))
        rows.append(jnp.zeros((AUX - len(rows), slots), f32))
        packed[place, slots : slots + AUX, :] = jnp.concatenate(rows, axis=0).astype(bf16)
    for copy in copies[3:]:
        copy.wait()


def load_kernel(*refs):
    sources, targets, sems = refs[:5], refs[5:10], refs[10]
    copies = [pltpu.make_async_copy(a, b, sems.at[i]) for i, (a, b) in enumerate(zip(sources, targets))]
    for copy in copies:
        copy.start()
    for copy in copies:
        copy.wait()


def pair_terms(near_pos, index, own_xyz, is_self, first_row, basis_count):
    n1 = float(basis_count - 1)
    gamma = 0.5 * n1 * n1
    delta = [near_pos[index, comp : comp + 1, :] - own_xyz[comp] for comp in range(3)]
    dist_sq = delta[0] * delta[0] + delta[1] * delta[1] + delta[2] * delta[2]
    dist_sq = jnp.minimum(dist_sq, 1.0)
    inside = 1.0 - dist_sq
    radius_sq = dist_sq + SOFTEN
    inverse = lax.rsqrt(radius_sq)
    radius = radius_sq * inverse
    gauss = jnp.exp2(radius_sq * (-gamma * LOG2E))
    step = jnp.exp2(radius * (n1 * LOG2E))
    if is_self:
        rows = first_row + lax.broadcasted_iota(jnp.int32, gauss.shape, 0)
        lanes = lax.broadcasted_iota(jnp.int32, gauss.shape, 1)
        gauss = jnp.where(rows == lanes, 0.0, gauss)
    part = inside * gauss
    weight = inside * part
    value_factor = part * (inside * -n1 - 2.0 * n1 / gamma)
    slope_factor = weight * (inverse * step)
    return step, weight, value_factor, slope_factor


def near_cell(aux, row, col, order):
    sx = jnp.where(order[0] == 0, 1.0, -1.0).astype(f32)
    sy = jnp.where(order[1] == 0, 1.0, -1.0).astype(f32)
    aux = aux.astype(f32)
    xyz = aux[0:3] + aux[3:6]
    x = xyz[0:1] + sx * float(1 - row)
    y = xyz[1:2] + sy * float(col)
    return [x, y, xyz[2:3]], xyz[0:1] < -0.5 * FAR, aux[6:7].astype(jnp.int32)


def strip_of(s):
    first = pl.multiple_of(s * STRIP, STRIP)
    return first, pl.ds(first, STRIP)


def stage(count, *steps):
    def body(s, carry):
        for step in steps:
            step(s)
        return carry

    lax.fori_loop(0, count, body, 0)


def fill_pairs(basis_count, slots, near_pos, own_pos, place, self_block, terms, weights, s):
    first, strip = strip_of(s)
    own_xyz = [own_pos[place, comp, strip, :] for comp in range(3)]
    for block in range(weights.shape[1] // slots):
        there = slice(block * slots, (block + 1) * slots)
        step, weight, value_factor, slope_factor = pair_terms(
            near_pos, block, own_xyz, block == self_block, first, basis_count
        )
        terms[0, strip, there] = step
        terms[1, strip, there] = value_factor
        terms[2, strip, there] = slope_factor
        for k in range(basis_count):
            rows = pl.ds(pl.multiple_of(first + k * slots, STRIP), STRIP)
            weights[rows, there] = weight.astype(bf16)
            if k < basis_count - 1:
                weight = weight * step


def carry_values(slots, value_t, gain_t, eye, near, here):
    near_feat, near_val, carried_t, onehot, projected, gains = near
    proj = dot_t(value_t, near_feat[here, :])
    gain = dot(gain_t, onehot[:, here])
    projected[:, here] = proj
    gains[:, here] = gain
    carried = (proj * gain).astype(bf16)
    carried_t[:, here] = carried
    for first in range(here.start, here.stop, slots):
        there = slice(first - here.start, first - here.start + slots)
        near_val[first : first + slots, :] = dot_t(eye, carried[:, there]).astype(bf16)


def chunk_of(s, size):
    return pl.ds(pl.multiple_of(s * size, size), size)


def early_kernel(
    basis_count, order, own, row_a, row_b, w_value, w_radial, type_gain,
    near_pos, own_pos, near_feat, near_val, carried_t, onehot, projected, gains,
    weights_b, weights_a, terms_b, terms_a, summed_b, summed_a, columns, value_t, gain_t,
):
    slots = near_feat.shape[1]
    strips = slots // STRIP
    chunk = basis_count * slots // strips
    weights, terms, summed = (weights_b, weights_a), (terms_b, terms_a), (summed_b, summed_a)
    for index in range(6):
        col, row = index // 3 + 1, index % 3
        ref = (row_a, own, row_b)[row]
        here = slice(index * slots, (index + 1) * slots)
        near_feat[here, :] = ref[col - 1, 0:slots, :]
        xyz, unused, types = near_cell(ref[col - 1, slots : slots + AUX, :], row, col, order)
        onehot[:, here] = onehot_rows(types, type_gain.shape[0], slots)
        for comp in range(3):
            near_pos[index, comp : comp + 1, :] = xyz[comp]
            if row == 1:
                line = jnp.where(unused, FAR, xyz[comp])
                own_pos[col - 1, comp] = jnp.broadcast_to(line, (slots, slots)).T
    near = (near_feat, near_val, carried_t, onehot, projected, gains)
    value_t[...] = w_value[...].astype(f32).T.astype(bf16)
    gain_t[...] = gain_columns(type_gain)
    carry_values(slots, value_t[...], gain_t[...], identity(slots), near, slice(0, 6 * slots))
    channels = w_value.shape[0]
    radial = [w_radial[k : k + 1, :] * math.exp(-0.5 * k * k) for k in range(basis_count)]
    radial_t = jnp.concatenate(radial + [jnp.zeros((channels - basis_count, channels), f32)], axis=0).T
    for k in range(basis_count):
        columns[k] = jnp.broadcast_to(radial_t[:, k : k + 1], (channels, slots))

    def sums(place, s):
        rows = chunk_of(s, chunk)
        summed[place][:, rows] = dot_t(carried_t[...], weights[place][rows, :])

    def pairs(place, s):
        fill_pairs(
            basis_count, slots, near_pos, own_pos, place, 3 * place + 1, terms[place], weights[place], s
        )

    run = functools.partial
    stage(strips, run(pairs, 0))
    stage(strips, run(sums, 0), run(pairs, 1))
    stage(strips, run(sums, 1))


def main_kernel(
    basis_count, order, col_a, col_b, cotangent, w_radial, w_out, columns, value_t, gain_t,
    own_pos, in_feat, in_carried_t, in_onehot, in_projected, in_gains,
    in_weights_b, in_weights_a, in_summed_b, in_summed_a,
    out_here, keep, pay_a, pay_b, fold_a, fold_b, own_acc,
    out_pos, ot_val, ot_terms_b, ot_terms_a, grad_agg,
    ot_feat, ot_carried_t, ot_onehot, ot_projected, ot_gains, products, whole,
    ot_weights_b, ot_weights_a, summed_b, summed_a, scaled_tb, scaled_ta, in_back, ot_back,
):
    slots, channels = cotangent.shape[2], cotangent.shape[3]
    type_count = gain_t.shape[1] // 3
    third = 3 * slots
    strips = slots // STRIP
    chunk = basis_count * slots // strips
    in_weights, ot_weights = (in_weights_b, in_weights_a), (ot_weights_b, ot_weights_a)
    ot_terms = (ot_terms_b, ot_terms_a)
    in_summed, summed = (in_summed_b, in_summed_a), (summed_b, summed_a)
    scaled_t = (scaled_tb, scaled_ta)
    for index in range(6):
        place, row = index // 3, index % 3
        ref = (col_b, col_a)[place]
        here = slice(index * slots, (index + 1) * slots)
        ot_feat[here, :] = ref[row, 0:slots, :]
        xyz, _, types = near_cell(ref[row, slots : slots + AUX, :], row, 3 * place, order)
        ot_onehot[:, here] = onehot_rows(types, type_count, slots)
        for comp in range(3):
            out_pos[index, comp : comp + 1, :] = xyz[comp]
    scale = [math.exp(-0.5 * k * k) for k in range(basis_count)]
    near = (ot_feat, ot_val, ot_carried_t, ot_onehot, ot_projected, ot_gains)
    carry_values(slots, value_t[...], gain_t[...], identity(slots), near, slice(0, 6 * slots))

    def outer(place):
        return slice(place * third, (place + 1) * third)

    def pairs(place, s):
        cells = out_pos.at[place * 3 : place * 3 + 3]
        fill_pairs(basis_count, slots, cells, own_pos, place, -1, ot_terms[place], ot_weights[place], s)

    def sums(place, s):
        rows = chunk_of(s, chunk)
        summed[place][:, rows] = in_summed[place][:, rows] + dot_t(
            ot_carried_t[:, outer(place)], ot_weights[place][rows, :]
        )

    def epilogue(place):
        aggregate_t = None
        for k in range(basis_count):
            term = summed[place][:, k * slots : (k + 1) * slots] * columns[k]
            aggregate_t = term if aggregate_t is None else aggregate_t + term
        agg_half = aggregate_t.T.astype(bf16)
        cell = jnp.where(order[1] == 0, place, 1 - place)
        pre_act = dot(agg_half, w_out[...])
        sig = jax.nn.sigmoid(pre_act)
        center = in_feat[(3 * place + 1) * slots : (3 * place + 2) * slots, :]
        out_here[place] = (center.astype(f32) + pre_act * sig).astype(bf16)
        grad_pre = (
            cotangent[0, cell].astype(f32) * sig * (1.0 + pre_act * (1.0 - sig))
        ).astype(bf16)
        agg_half = dot_t(grad_pre, w_out[...]).astype(bf16)
        grad_agg[place] = agg_half
        agg_t = agg_half.astype(f32).T
        for k in range(basis_count):
            here = slice(k * slots, (k + 1) * slots)
            scaled_t[place][:, here] = (agg_t * columns[k]).astype(bf16)
            product = agg_t * summed[place][:, here]
            products[:, here] = product if place == 0 else products[:, here] + product
        return dot(aggregate_t.astype(bf16), grad_pre)

    def value_grads(place):
        inner = dot(scaled_t[place][...], in_weights[place][...])
        in_back[...] = inner if place == 0 else in_back[...] + inner
        ot_back[:, outer(place)] = dot(scaled_t[place][...], ot_weights[place][...])

    run = functools.partial
    stage(strips, run(pairs, 0))
    stage(strips, run(sums, 0), run(pairs, 1))
    for s in range(strips):
        sums(1, s)
    wout = epilogue(0)
    value_grads(0)
    wout = wout + epilogue(1)
    value_grads(1)

    wvalue = ggain = None
    for back, feat, onehot, projected, gains in (
        (in_back, in_feat, in_onehot, in_projected, in_gains),
        (ot_back, ot_feat, ot_onehot, ot_projected, ot_gains),
    ):
        half = (back[...] * gains[...]).astype(bf16)
        wvalue_part = dot(half, feat[...])
        ggain_part = dot_t((back[...] * projected[...]).astype(bf16), onehot[0:type_count, :])
        wvalue = wvalue_part if wvalue is None else wvalue + wvalue_part
        ggain = ggain_part if ggain is None else ggain + ggain_part
    ggain = jnp.concatenate([ggain, jnp.zeros((channels, slots - ggain.shape[1]), f32)], axis=1).T
    group = lax.broadcasted_iota(jnp.int32, (basis_count, basis_count * slots), 1) // slots
    mine = lax.broadcasted_iota(jnp.int32, (basis_count, basis_count * slots), 0)
    select = jnp.where(group == mine, 1.0, 0.0).astype(bf16)
    wradial = dot_t(select, products[...].astype(bf16))
    wradial = jnp.concatenate([wradial[k : k + 1] * scale[k] for k in range(basis_count)], axis=0)
    pad = 2 * keep.shape[0] - 2 * channels - type_count - basis_count
    tail = [ggain[0:type_count], wradial] + ([jnp.zeros((pad, channels), f32)] if pad else [])
    full = jnp.concatenate([wvalue.T, wout] + tail, axis=0).astype(bf16)
    rows = keep.shape[0]
    whole[0] = full[0:rows]
    whole[1] = full[rows : 2 * rows]
    keep[...] = whole[order[0]]
    for ref in (pay_a, pay_b):
        ref[0:rows, :] = whole[1 - order[0]]
    for col in range(4):
        for row in range(3):
            inner = col in (1, 2)
            local = (col - 1) * 3 + row if inner else (0 if col == 0 else 3) + row
            back = (in_back if inner else ot_back)[:, local * slots : (local + 1) * slots]
            if row == 1:
                own_acc[col] = back
            elif inner:
                ref = fold_a if row == 0 else fold_b
                ref[(col - 1) * slots : col * slots, :] = back.astype(bf16)
            else:
                ref = pay_a if row == 0 else pay_b
                base = rows + (0 if col == 0 else slots)
                ref[base : base + slots, :] = back.astype(bf16)


def pulls_kernel(
    basis_count, order, in_pos, own_pos, in_val, in_terms_b, in_terms_a, out_pos, ot_val,
    ot_terms_b, ot_terms_a, grad_agg, w_radial,
    lines,
    scaled_b, scaled_a, in_grad_b, in_grad_a, ot_grad_b, ot_grad_a, pull_own, pull_far,
):
    slots = in_pos.shape[2]
    third = 3 * slots
    strips = slots // STRIP
    chunk = basis_count * slots // strips
    in_terms, ot_terms = (in_terms_b, in_terms_a), (ot_terms_b, ot_terms_a)
    scaled = (scaled_b, scaled_a)
    in_grad, ot_grad = (in_grad_b, in_grad_a), (ot_grad_b, ot_grad_a)

    def weight_grads(place, s):
        rows = chunk_of(s, chunk)
        in_grad[place][rows, :] = dot_t(scaled[place][rows, :], in_val[...])
        outer = slice(place * third, (place + 1) * third)
        ot_grad[place][rows, :] = dot_t(scaled[place][rows, :], ot_val[outer, :])

    def pulls(place, s):
        first, strip = strip_of(s)
        own_xyz = [own_pos[place, comp, strip, :] for comp in range(3)]
        total = [jnp.zeros((STRIP, slots), f32) for _ in range(3)]
        for block in range(9):
            inner = block < 6
            grad = (in_grad if inner else ot_grad)[place]
            terms = (in_terms if inner else ot_terms)[place]
            cells = in_pos if inner else out_pos
            cell = block if inner else place * 3 + block - 6
            index = block if inner else 6 + cell
            local = block if inner else block - 6
            there = slice(local * slots, (local + 1) * slots)

            def grad_of(k):
                rows = pl.ds(pl.multiple_of(first + k * slots, STRIP), STRIP)
                return grad[rows, there]

            step = terms[0, strip, there]
            value = grad_of(basis_count - 1)
            slope = None
            for k in range(basis_count - 2, -1, -1):
                slope = value if slope is None else value + step * slope
                value = grad_of(k) + step * value
            pull = terms[1, strip, there] * value + terms[2, strip, there] * slope
            for comp in range(3):
                force = pull * (cells[cell, comp : comp + 1, :] - own_xyz[comp])
                total[comp] = total[comp] + force
                pull_far[index, comp] += (force[0:8] + force[8:16]) + (force[16:24] + force[24:32])
        for comp in range(3):
            pull_own[place, comp, strip, :] = total[comp]

    run = functools.partial
    pull_far[...] = jnp.zeros_like(pull_far)
    for place in range(2):
        agg = grad_agg[place].astype(f32)
        for k in range(basis_count):
            factor = w_radial[k : k + 1, :] * math.exp(-0.5 * k * k)
            scaled[place][k * slots : (k + 1) * slots, :] = (agg * factor).astype(bf16)
        if place == 0:
            for s in range(strips):
                weight_grads(0, s)
    stage(strips, run(weight_grads, 1), run(pulls, 0))
    stage(strips, run(pulls, 1))
    force = float(basis_count - 1)
    rows = []
    for col in range(4):
        for row in range(3):
            inner = col in (1, 2)
            local = (col - 1) * 3 + row if inner else 6 + (0 if col == 0 else 3) + row
            for comp in range(3):
                line = jnp.sum(pull_far[local, comp], axis=0, keepdims=True)
                if row == 1 and inner:
                    line = line - jnp.sum(pull_own[col - 1, comp].T, axis=0, keepdims=True)
                rows.append(line * (force * HZ if comp == 2 else force))
            rows.append(jnp.zeros((1, slots), f32))
        rows.append(jnp.zeros((4, slots), f32))
    lines[...] = jnp.concatenate(rows, axis=0)


def cells_kernel(
    order, own, got_a, got_b, far, near, cotangent, w_value, gains, grad_feat
):
    slots = own.shape[2]
    for place in range(2):
        cell = jnp.where(order[1] == 0, place, 1 - place)
        here = slice(place * slots, (place + 1) * slots)
        got = far[0:slots, :] if place == 0 else near[near.shape[0] - LINES - slots : near.shape[0] - LINES, :]
        total = own[place + 1] + add(got_a[here, :], got_b[here, :]) + got.astype(f32)
        half = (total * gains[:, (3 * place + 1) * slots : (3 * place + 2) * slots]).astype(bf16)
        grad_feat[0, cell] = (cotangent[0, cell].astype(f32) + dot(w_value[...], half).T).astype(bf16)


def emit_kernel(order, out_here, out_feat):
    for place in range(2):
        out_feat[0, jnp.where(order[1] == 0, place, 1 - place)] = out_here[place]


def finish_kernel(order, mine, other, feat, lines, grad_feat, grad_pos, wvalue, wradial, ggain, wout):
    grad_feat[...] = feat[...]
    for place in range(2):
        cell = jnp.where(order[1] == 0, place, 1 - place)
        for comp in range(3):
            row = 4 * place + comp
            grad_pos[0, comp, pl.ds(cell, 1), :] = lines[row : row + 1, :]
    first = order[0] == 0
    low = jnp.where(first, mine[...], other[...])
    high = jnp.where(first, other[...], mine[...])
    total = jnp.concatenate([low, high], axis=0)
    base = 0
    for ref in (wvalue, wout, ggain, wradial):
        ref[...] = total[base : base + ref.shape[0]]
        base += ref.shape[0]


def edges(axis):
    count = lax.axis_size(axis)
    assert count % 2 == 0 and count > 2 and count & (count - 1) == 0
    even = [(i, i ^ 1) for i in range(count)]
    odd = [(i, (i + 1) % count if i % 2 else (i - 1) % count) for i in range(count)]
    return even, odd


def across(axis, step):
    return [(i, i ^ step) for i in range(lax.axis_size(axis))]


def add(a, b):
    return a.astype(f32) + b.astype(f32)


def on_device(
    features, positions, bead_types, cell_counts, w_value, w_radial, type_gain, w_out, cotangent
):
    row_count, col_count, slots, channels = features.shape
    basis_count, type_count = w_radial.shape[0], type_gain.shape[0]
    assert row_count == 1 and col_count == 2 and slots == channels == LANES
    assert 3 * type_count <= slots and type_count % 8 == 0 and basis_count == 8
    order = jnp.stack([lax.axis_index("gx") % 2, lax.axis_index("gy") % 2]).astype(jnp.int32)
    smem = pl.BlockSpec(memory_space=pltpu.SMEM)
    vmem = pl.BlockSpec(memory_space=pltpu.VMEM)
    x_even, x_odd = edges("gx")
    y_even, y_odd = edges("gy")
    size = slots + AUX
    inner, outer, tall = 6 * slots, 3 * slots, basis_count * slots
    rows = -(-(2 * channels + type_count + basis_count) // 32) * 16
    kinds = 3 * type_count
    shape = jax.ShapeDtypeStruct

    def call(kernel, mib, out_shape, arrays, scratch=()):
        return pl.pallas_call(
            kernel,
            out_shape=out_shape,
            in_specs=[smem] + [vmem] * len(arrays),
            out_specs=jax.tree.map(lambda _: vmem, out_shape),
            scratch_shapes=list(scratch),
            compiler_params=pltpu.CompilerParams(vmem_limit_bytes=mib * 2**20),
        )(order, *arrays)

    hbm = pl.BlockSpec(memory_space=pltpu.HBM)
    small = pltpu.CompilerParams(vmem_limit_bytes=4 * 2**20)

    def in_hbm(*arrays):
        return [pltpu.with_memory_space_constraint(a, pltpu.HBM) for a in arrays]

    packed = pl.pallas_call(
        pack_kernel,
        out_shape=shape((2, size, channels), bf16),
        in_specs=[smem] + [hbm] * 4,
        out_specs=vmem,
        scratch_shapes=[
            pltpu.SMEM(cell_counts.shape, jnp.int32),
            pltpu.VMEM((row_count, 3, col_count, slots), f32),
            pltpu.VMEM(bead_types.shape, jnp.int32),
            pltpu.SemaphoreType.DMA((5,)),
        ],
        compiler_params=small,
        name="pack",
    )(order, *in_hbm(cell_counts, features, jnp.swapaxes(positions, 1, 2), bead_types))
    later = (cotangent, w_value, w_radial, type_gain, w_out)
    cotangent, w_value, w_radial, type_gain, w_out = pl.pallas_call(
        load_kernel,
        out_shape=tuple(shape(a.shape, a.dtype) for a in later),
        in_specs=[hbm] * 5,
        out_specs=(vmem,) * 5,
        scratch_shapes=[pltpu.SemaphoreType.DMA((5,))],
        compiler_params=small,
        name="load",
    )(*in_hbm(*later))
    row_b = lax.ppermute(packed, "gx", x_odd)
    row_a = lax.ppermute(packed, "gx", x_even)
    col_b = lax.ppermute(jnp.stack([row_a[0], packed[0], row_b[0]]), "gy", y_odd)
    col_a = lax.ppermute(jnp.stack([row_a[1], packed[1], row_b[1]]), "gy", y_even)
    early = call(
        functools.partial(early_kernel, basis_count), 8,
        (
            shape((6, 8, slots), f32),
            shape((2, 3, slots, slots), f32),
            shape((inner, channels), bf16),
            shape((inner, channels), bf16),
            shape((channels, inner), bf16),
            shape((kinds, inner), bf16),
            shape((channels, inner), f32),
            shape((channels, inner), f32),
        )
        + (shape((tall, inner), bf16),) * 2
        + (shape((3, slots, inner), f32),) * 2
        + (shape((channels, tall), f32),) * 2
        + (
            shape((basis_count, channels, slots), f32),
            shape((channels, channels), bf16),
            shape((channels, kinds), bf16),
        ),
        (packed, row_a, row_b, w_value, w_radial, type_gain),
    )
    (
        in_pos, own_pos, in_feat, in_val, in_carried_t, in_onehot, in_projected, in_gains,
        in_weights_b, in_weights_a, in_terms_b, in_terms_a, in_summed_b, in_summed_a,
        columns, value_t, gain_t,
    ) = early
    (
        out_here, keep, pay_a, pay_b, fold_a, fold_b, own_acc,
        out_pos, ot_val, ot_terms_b, ot_terms_a, grad_agg,
    ) = call(
        functools.partial(main_kernel, basis_count), 16,
        (
            shape((2, slots, channels), bf16),
            shape((rows, channels), bf16),
            shape((rows + 2 * channels, slots), bf16),
            shape((rows + 2 * channels, slots), bf16),
            shape((2 * channels, slots), bf16),
            shape((2 * channels, slots), bf16),
            shape((4, channels, slots), f32),
            shape((6, 8, slots), f32),
            shape((2 * outer, channels), bf16),
        )
        + (shape((3, slots, outer), f32),) * 2
        + (shape((2, slots, channels), bf16),),
        (
            col_a, col_b, cotangent, w_radial, w_out, columns, value_t, gain_t,
            own_pos, in_feat, in_carried_t, in_onehot, in_projected, in_gains,
            in_weights_b, in_weights_a, in_summed_b, in_summed_a,
        ),
        [
            pltpu.VMEM((2 * outer, channels), bf16),
            pltpu.VMEM((channels, 2 * outer), bf16),
            pltpu.VMEM((kinds, 2 * outer), bf16),
            pltpu.VMEM((channels, 2 * outer), f32),
            pltpu.VMEM((channels, 2 * outer), f32),
            pltpu.VMEM((channels, tall), f32),
            pltpu.VMEM((2, rows, channels), bf16),
        ]
        + [pltpu.VMEM((tall, outer), bf16)] * 2
        + [pltpu.VMEM((channels, tall), f32)] * 2
        + [pltpu.VMEM((channels, tall), bf16)] * 2
        + [pltpu.VMEM((channels, inner), f32), pltpu.VMEM((channels, 2 * outer), f32)],
    )
    got_b = lax.ppermute(pay_b, "gx", x_odd)
    got_a = lax.ppermute(pay_a, "gx", x_even)
    if len(x_even) == 4:
        other = lax.ppermute(keep, "gx", across("gx", 2))
        total = add(keep, got_a[:rows]) + add(other, got_b[:rows])
    else:
        total = add(keep, got_a[:rows])
        step = 2
        while step < len(x_even):
            part = total.astype(bf16)
            total = add(part, lax.ppermute(part, "gx", across("gx", step)))
            step *= 2
    lines = call(
        functools.partial(pulls_kernel, basis_count), 20, shape((4 * LINES, slots), f32),
        (
            in_pos, own_pos, in_val, in_terms_b, in_terms_a, out_pos, ot_val,
            ot_terms_b, ot_terms_a, grad_agg, w_radial,
        ),
        [pltpu.VMEM((tall, channels), bf16)] * 2
        + [pltpu.VMEM((tall, inner), f32)] * 2
        + [pltpu.VMEM((tall, outer), f32)] * 2
        + [pltpu.VMEM((2, 3, slots, slots), f32), pltpu.VMEM((12, 3, 8, slots), f32)],
    )
    part = total.astype(bf16)
    corner_b = own_acc[0] + add(got_a[rows : rows + channels], got_b[rows : rows + channels])
    corner_a = own_acc[3] + add(got_a[rows + channels :], got_b[rows + channels :])
    sent = lines.astype(bf16)
    got = lax.ppermute(
        jnp.concatenate([part, corner_a.astype(bf16), sent[3 * LINES :]]), "gy", y_even
    )
    far = lax.ppermute(jnp.concatenate([corner_b.astype(bf16), sent[:LINES]]), "gy", y_odd)
    lines_here = lines[LINES : 3 * LINES]
    sent = lines_here.astype(bf16)
    own_b = lax.ppermute(jnp.concatenate([fold_b, sent]), "gx", x_odd)
    own_a = lax.ppermute(jnp.concatenate([fold_a, sent]), "gx", x_even)
    total = add(part, got[:rows])
    step = 2
    while step < len(y_even):
        part = total.astype(bf16)
        got_far = lax.ppermute(part, "gy", across("gy", step))
        total = add(part, got_far)
        step *= 2
    sent = jnp.concatenate([far[channels:], got[rows + channels :]])
    more_b = lax.ppermute(sent, "gx", x_odd)
    more_a = lax.ppermute(sent, "gx", x_even)
    back_a = add(own_a[2 * channels :], more_a)
    back_b = add(own_b[2 * channels :], more_b)
    lines_here = lines_here + sent.astype(f32)
    pos = jnp.concatenate(
        [
            lines_here[base + 4 : base + 8] + (back_a[base : base + 4] + back_b[base + 8 : base + 12])
            for base in (0, LINES)
        ]
    )
    out_feat = call(emit_kernel, 4, shape(features.shape, bf16), (out_here,))
    half = lax.ppermute(total, "gx", x_even)
    grad_feat = call(
        cells_kernel, 4, shape(features.shape, bf16),
        (own_acc, own_a, own_b, far, got, cotangent, w_value, in_gains),
    )
    grad_feat, grad_pos, wvalue, wradial, ggain, wout = call(
        finish_kernel, 4,
        (
            shape(grad_feat.shape, bf16),
            shape((row_count, 3, col_count, slots), f32),
            shape((channels, channels), f32),
            shape((basis_count, channels), f32),
            shape((type_count, channels), f32),
            shape((channels, channels), f32),
        ),
        (total, half, grad_feat, pos),
    )
    return out_feat, grad_feat, jnp.swapaxes(grad_pos, 1, 2), wvalue, wradial, ggain, wout


def solution(mesh):
    cell = P(("frame", "gx"), "gy", None, None)

    return jax.shard_map(
        on_device,
        mesh=mesh,
        in_specs=(
            cell, cell, P(("frame", "gx"), "gy", None), P(("frame", "gx"), "gy"),
            P(), P(), P(), P(), cell,
        ),
        out_specs=(cell, cell, cell) + (P("frame", None),) * 4,
        check_vma=False,
    )
```
